32 devices in a mesh: dp: 8 (over z, y), tensor: 4 (over x, core).
Axes of the slice: x: 2, y: 2, z: 4, core: 2. Of those that a mesh axis runs over, the one named last changes fastest.
Arguments:
- tokens: bfloat16 [16384, 768], P('dp'), may hold values from -8 to 8
- lengths: int32 [8, 16], P('dp'), may hold values from 1 to 1024, 2048 in all within a row
- attn_gain: float32 [768], replicated, may hold values from 0.1 to 1.9
- qkv_weight: bfloat16 [768, 3, 768], P('dp', None, 'tensor'), may hold values from -0.21875 to 0.21875
- out_weight: bfloat16 [768, 768], P('tensor', 'dp'), may hold values from -0.625 to 0.625
- mlp_gain: float32 [768], replicated, may hold values from 0.1 to 1.9
- up_weight: bfloat16 [768, 2, 1152], P('dp', None, 'tensor'), may hold values from -0.21875 to 0.21875
- down_weight: bfloat16 [1152, 768], P('tensor', 'dp'), may hold values from -0.25 to 0.25
- cotangent: bfloat16 [16384, 768], P('dp'), may hold values from -8 to 8
Outputs:
- output: bfloat16 [16384, 768], P('dp')
- tokens_grad: float32 [16384, 768], P('dp')
- attn_gain_grad: float32 [768], P('dp')
- qkv_grad: float32 [768, 3, 768], P('dp', None, 'tensor')
- out_grad: float32 [768, 768], P('tensor', 'dp')
- mlp_gain_grad: float32 [768], P('dp')
- up_grad: float32 [768, 2, 1152], P('dp', None, 'tensor')
- down_grad: float32 [1152, 768], P('tensor', 'dp')
The draws below stay inside these ranges and needn't reach their ends.
Inputs may be any that keep to these rules, and one draw needn't show every extreme that they name: Each row's 16 document lengths sum to 2048, and the longest of every row is exactly 1024.
All inputs are finite; a program needn't handle non-finite values.
Results may differ from the reference program's by a relative error of at most 0.02.
Values may be sent and summed in bfloat16 or wider, within the bound.
No kernel may reach another device: no remote copies, remote signals or barrier semaphores. Data moves between devices by JAX's collectives and lax.ppermute only.
A program may use at most 192 MiB of HBM per device.

```python
import math
import jax
import jax.numpy as jnp
import numpy as np
from jax import lax

D = 768
HEADS = 12
HD = 64
FF = 1152
ROW_TOK = 2048
DOCS = 16
BLOCK = 512
ROWS = 8
TOKENS = 16384
N_TENSOR = 4


def with_spikes(drawn, key, source, target, shards_of, factor):
    owner, partner = [(jnp.arange(drawn.shape[dim]) // (drawn.shape[dim] // shards_of)).reshape([-1 if axis == dim else 1 for axis in range(drawn.ndim)]) for dim in (source, target)]
    chosen = jax.random.permutation(key, shards_of)[partner]
    strong = (owner == chosen) | (owner == (partner + shards_of // 2) % shards_of)
    return jnp.where(strong, factor * drawn, drawn)


def block_levels(rng, shape, shards, least, largest):
    factor_of, own = 1.0, jax.random.fold_in(rng, 6)
    for dim, shards_of in shards:
        heights = jnp.exp(jax.random.uniform(jax.random.fold_in(own, dim), (shards_of,), jnp.float32, least / len(shards), largest / len(shards)))
        factor_of = factor_of * jnp.repeat(heights, shape[dim] // shards_of).reshape([-1 if axis == dim else 1 for axis in range(len(shape))])
    return factor_of


def profile(amount, total, bound, skew):
    weights = [(1 << 20) // math.isqrt(grade ** skew) + 1 for grade in range(2, amount + 1)]
    spare, counts = total - bound - (amount - 1), [1] * (amount - 1)
    while spare > 0:
        candidates = [i for i in range(amount - 1) if counts[i] < bound]
        pool, remaining = sum([weights[i] for i in candidates]), spare
        for i in candidates:
            more = min(bound - counts[i], max(1, remaining * weights[i] // pool), spare)
            counts[i] = counts[i] + more
            spare = spare - more
    return np.array([bound] + counts)


def ragged_sizes(rng, amount, total, limit, slope):
    if amount == 2:
        one = jax.random.randint(rng, (), max(1, total - limit), min(limit, total - 1) + 1)
        return jnp.stack([one, total - one])
    tallies = jnp.asarray(profile(amount, total, limit, slope), jnp.int32)
    pairs = (amount - 1) // 2
    source_of, receiver = tallies[1:1 + 2 * pairs:2], tallies[2:2 + 2 * pairs:2]
    margin = jnp.minimum(source_of - 1, limit - receiver)
    shifted = jax.random.randint(jax.random.fold_in(rng, 1), (pairs,), 0, 1 << 20) % (margin + 1)
    tallies = tallies.at[1:1 + 2 * pairs:2].set(source_of - shifted).at[2:2 + 2 * pairs:2].set(receiver + shifted)
    return tallies[jax.random.permutation(jax.random.fold_in(rng, 2), amount)]


def noise(own_key, shape, deviation, reach, split=(), kind=jnp.bfloat16):
    entries = deviation * jax.random.normal(own_key, shape, jnp.float32)
    if split:
        entries = entries * block_levels(own_key, shape, split, -0.22, 0.18)
    return jnp.clip(entries, -reach, reach).astype(kind)


def heavy_noise(key, extent, deviation, reach, cuts, heavy, kind=jnp.bfloat16):
    drawn = deviation * jax.random.normal(key, extent, jnp.float32)
    if cuts:
        drawn = drawn * block_levels(key, extent, cuts, -0.22, 0.18)
    return jnp.clip(with_spikes(drawn, jax.random.fold_in(key, 3), *heavy), -reach, reach).astype(kind)


def setup_inputs(seed: int = 0) -> dict:
    key_of = jax.random.split(jax.random.key(seed), 10)
    tokens = heavy_noise(key_of[0], (TOKENS, D), 1.0, 8.0, ((0, 8),), (0, 1, 8, 2.0))
    lengths = jax.vmap(lambda own: ragged_sizes(own, DOCS, ROW_TOK, ROW_TOK // 2, 2))(jax.random.split(key_of[1], ROWS)).reshape((ROWS, DOCS)).astype(jnp.int32)
    attn_gain = jnp.clip(1.0 + 0.18 * jax.random.normal(key_of[2], (D,), jnp.float32), 0.1, 1.9)
    qkv_weight = noise(key_of[3], (D, 3, HEADS * HD), D ** -0.5, 0.21875, ((0, 8), (2, 4)))
    out_weight = noise(key_of[4], (HEADS * HD, D), (D // 8) ** -0.5, 0.625, ((0, 4), (1, 8)))
    mlp_gain = jnp.clip(1.0 + 0.18 * jax.random.normal(key_of[5], (D,), jnp.float32), 0.1, 1.9)
    up_weight = noise(key_of[6], (D, 2, FF), D ** -0.5, 0.21875, ((0, 8), (2, 4)))
    down_weight = noise(key_of[7], (FF, D), (FF // 2) ** -0.5, 0.25, ((0, 4), (1, 8)))
    cotangent = heavy_noise(key_of[8], (TOKENS, D), 1.0, 8.0, ((0, 8),), (0, 1, 8, 2.0))
    return dict(tokens=tokens, lengths=lengths, attn_gain=attn_gain, qkv_weight=qkv_weight, out_weight=out_weight, mlp_gain=mlp_gain, up_weight=up_weight, down_weight=down_weight, cotangent=cotangent)


eps_norm = 1e-05
theta_base = 160000.0
highest = lax.Precision.HIGHEST

@jax.custom_vjp
def low(v):
    return lax.optimization_barrier(v.astype(jnp.bfloat16)).astype(jnp.float32)

@jax.custom_vjp
def low_back(v):
    return v

def low_keep(v):
    return (low(v), None)

def low_pass(kept, grad):
    return (grad,)

def back_keep(v):
    return (v, None)

def back_low(kept, grad):
    return (low(grad),)
low.defvjp(low_keep, low_pass)
low_back.defvjp(back_keep, back_low)

def row_layout(row_lengths, tok_count):
    doc_ends = jnp.cumsum(row_lengths, dtype=jnp.int32)
    tok_place = jnp.arange(tok_count, dtype=jnp.int32)
    passed = tok_place[:, None] >= doc_ends[None, :]
    segment = lax.optimization_barrier(jnp.sum(passed.astype(jnp.int32), axis=1, dtype=jnp.int32))
    doc_start = lax.optimization_barrier(jnp.sum(jnp.where(passed, row_lengths[None, :], 0), axis=1, dtype=jnp.int32))
    return (segment, tok_place - doc_start)

def rotary_tables(position, head_width):
    half_width = head_width // 2
    freq_index = jnp.arange(half_width, dtype=jnp.float32)
    inv_freq = jnp.exp(freq_index * (-2.0 * math.log(theta_base) / head_width))
    angles = position.astype(jnp.float32)[:, None] * inv_freq[None, :]
    angles = jnp.concatenate([angles, angles], axis=1)
    return (jnp.cos(angles), jnp.sin(angles))

def rotate(vector, cosine, sine_table):
    half_width = vector.shape[-1] // 2
    turned = jnp.concatenate([-vector[..., half_width:], vector[..., :half_width]], axis=-1)
    return vector * cosine[:, None, :] + turned * sine_table[:, None, :]

def layer_norm(vector, gain_vec):
    row_mean = lax.optimization_barrier(jnp.mean(vector, axis=-1, keepdims=True))
    centred = vector - row_mean
    spread = lax.optimization_barrier(jnp.mean(centred * centred, axis=-1, keepdims=True))
    return centred * lax.rsqrt(spread + eps_norm) * gain_vec

def forward_row(row_in, attn_gain, qkv_weight, out_weight, mlp_gain, up_weight, down_weight, segment, cosine, sine_table):
    tok_count = row_in.shape[0]
    head_cols = HEADS * HD // N_TENSOR
    hidden_cols = FF // N_TENSOR
    score_scale = HD ** (-0.5)
    h_one = low(layer_norm(row_in, attn_gain))
    pieces = []
    for group_id in range(N_TENSOR):
        taken = low_back(h_one)
        piece = jnp.einsum('td,dcf->tcf', taken, qkv_weight[:, :, group_id * head_cols:(group_id + 1) * head_cols], precision=highest)
        pieces.append(low_back(piece))
    qkv_rows = jnp.concatenate(pieces, axis=2)
    queries = low(rotate(qkv_rows[:, 0].reshape(tok_count, HEADS, HD), cosine, sine_table))
    key_rows = low(rotate(qkv_rows[:, 1].reshape(tok_count, HEADS, HD), cosine, sine_table))
    value_rows = low(qkv_rows[:, 2].reshape(tok_count, HEADS, HD))
    block_count = tok_count // BLOCK

    def one_block(block_item):
        query_block, seg_block = block_item
        scores = low_back(jnp.einsum('qhd,khd->hqk', query_block, key_rows, precision=highest) * score_scale)
        same_doc = (seg_block[:, None] == segment[None, :])[None]
        masked = jnp.where(same_doc, scores, -1e+30)
        row_max = lax.optimization_barrier(jnp.max(masked, axis=2, keepdims=True))
        expos = jnp.exp(masked - row_max)
        probabilities = low(expos / lax.optimization_barrier(jnp.sum(expos, axis=2, keepdims=True)))
        return jnp.einsum('hqk,khd->qhd', probabilities, value_rows, precision=highest)
    attended = lax.map(jax.checkpoint(one_block), (queries.reshape(block_count, BLOCK, HEADS, HD), segment.reshape(block_count, BLOCK)))
    attended = low_back(low(attended.reshape(tok_count, HEADS * HD)))
    attn_branch = jnp.zeros((tok_count, D), jnp.float32)
    for group_id in range(N_TENSOR):
        part_sum = jnp.dot(attended[:, group_id * head_cols:(group_id + 1) * head_cols], out_weight[group_id * head_cols:(group_id + 1) * head_cols], precision=highest)
        attn_branch = attn_branch + low(part_sum)
    mid = row_in + low_back(attn_branch)
    h_two = low(layer_norm(mid, mlp_gain))
    mlp_branch = jnp.zeros((tok_count, D), jnp.float32)
    for group_id in range(N_TENSOR):
        taken = low_back(h_two)
        gate_up = low_back(jnp.einsum('td,dcf->tcf', taken, up_weight[:, :, group_id * hidden_cols:(group_id + 1) * hidden_cols], precision=highest))
        hidden = low_back(low(jax.nn.gelu(gate_up[:, 0], approximate=False) * gate_up[:, 1]))
        part_sum = jnp.dot(hidden, down_weight[group_id * hidden_cols:(group_id + 1) * hidden_cols], precision=highest)
        mlp_branch = mlp_branch + low(part_sum)
    return mid + low_back(mlp_branch)

def reference(tokens, lengths, attn_gain, qkv_weight, out_weight, mlp_gain, up_weight, down_weight, cotangent):
    weights = (attn_gain.astype(jnp.float32), qkv_weight.astype(jnp.float32), out_weight.astype(jnp.float32), mlp_gain.astype(jnp.float32), up_weight.astype(jnp.float32), down_weight.astype(jnp.float32))
    rows_in = tokens.astype(jnp.float32).reshape(ROWS, ROW_TOK, D)
    rows_cot = cotangent.astype(jnp.float32).reshape(ROWS, ROW_TOK, D)

    def row_step(totals, row_item):
        row_in, row_lengths, row_cot = row_item
        segment, position = row_layout(row_lengths, ROW_TOK)
        cosine, sine_table = rotary_tables(position, HD)

        def forward(row_value, gain_one, weight_qkv, weight_out, gain_two, weight_up, weight_down):
            return forward_row(row_value, gain_one, weight_qkv, weight_out, gain_two, weight_up, weight_down, segment, cosine, sine_table)
        result, pull_back = jax.vjp(forward, row_in, weights[0], weights[1], weights[2], weights[3], weights[4], weights[5])
        grads = pull_back(row_cot)
        totals = tuple((acc_grad + new_grad for acc_grad, new_grad in zip(totals, grads[1:])))
        return (totals, (result.astype(jnp.bfloat16), grads[0]))
    start_totals = tuple((jnp.zeros_like(weight_one) for weight_one in weights))
    totals, (output, grad_tokens) = lax.scan(row_step, start_totals, (rows_in, lengths, rows_cot))
    return (output.reshape(TOKENS, D), grad_tokens.reshape(TOKENS, D), totals[0], totals[1], totals[2], totals[3], totals[4], totals[5])
```

```python
import math

import jax
import jax.numpy as jnp
from jax import lax
from jax.experimental import pallas as pl
from jax.experimental.pallas import tpu as pltpu
from jax.sharding import PartitionSpec as P

HD = 64


eps_norm = 1e-05
theta_base = 160000.0


def cut_along(value, dim, count):
    shape = value.shape
    pieces = value.reshape(*shape[:dim], count, shape[dim] // count, *shape[dim + 1 :])
    return jnp.moveaxis(pieces, dim, 0)


def sent_and_summed(value, axis, dim):
    pieces = cut_along(value, dim, lax.axis_size(axis))
    arrived = lax.all_to_all(pieces, axis, split_axis=0, concat_axis=0, tiled=True)
    return arrived.astype(jnp.float32).sum(axis=0)


def in_one_piece(arrays, axis, dim, along):
    widths = [math.prod(a.shape[along:]) for a in arrays]
    both = jnp.concatenate(
        [a.reshape(*a.shape[:along], w) for a, w in zip(arrays, widths)], axis=along
    )
    result = sent_and_summed(both, axis, dim)
    pieces = jnp.split(result, [sum(widths[:k]) for k in range(1, len(widths))], axis=along)
    return tuple(
        (b.reshape(*result.shape[:along], *a.shape[along:]) for a, b in zip(arrays, pieces))
    )


def in_one_piece_2(arrays, axis, dim, along):
    widths = [a.shape[along] for a in arrays]
    both = jnp.concatenate(arrays, axis=along)
    result = sent_and_summed(both, axis, dim)
    return tuple(jnp.split(result, [sum(widths[:k]) for k in range(1, len(widths))], axis=along))


def row_layout(row_lengths, tok_count):
    doc_ends = jnp.cumsum(row_lengths, dtype=jnp.int32)
    tok_place = jnp.arange(tok_count, dtype=jnp.int32)
    passed = tok_place[:, None] >= doc_ends[None, :]
    segment = jnp.sum(passed.astype(jnp.int32), axis=1, dtype=jnp.int32)
    doc_start = jnp.sum(jnp.where(passed, row_lengths[None, :], 0), axis=1, dtype=jnp.int32)
    return (segment, tok_place - doc_start)


def tile_ranges(row_lengths, tok_count):
    ends = jnp.cumsum(row_lengths, dtype=jnp.int32)
    starts = ends - row_lengths
    begin = jnp.arange(tok_count // TILE, dtype=jnp.int32)[:, None] * TILE
    touched = (ends[None, :] > begin) & (starts[None, :] < begin + TILE)
    low = jnp.min(jnp.where(touched, starts[None, :], tok_count), axis=1)
    high = jnp.max(jnp.where(touched, ends[None, :], 0), axis=1)
    return (low // TILE, (high + TILE - 1) // TILE)


def rotary_tables(position, head_width):
    half_width = head_width // 2
    freq_index = jnp.arange(half_width, dtype=jnp.float32)
    inv_freq = jnp.exp(freq_index * (-2.0 * math.log(theta_base) / head_width))
    angles = position.astype(jnp.float32)[:, None] * inv_freq[None, :]
    cosine, sine = jnp.cos(angles), jnp.sin(angles)
    return (jnp.concatenate([cosine, cosine], axis=1), jnp.concatenate([-sine, sine], axis=1))


def normalize(vector):
    row_mean = jnp.mean(vector, axis=-1, keepdims=True)
    centred = vector - row_mean
    spread = jnp.mean(centred * centred, axis=-1, keepdims=True)
    factor = lax.rsqrt(spread + eps_norm)
    return (centred * factor, factor)


def norm_back(grad_norm_out, normed, factor, gain_vec):
    grad_normed = grad_norm_out * gain_vec
    first_mean = jnp.mean(grad_normed, axis=-1, keepdims=True)
    second_mean = jnp.mean(grad_normed * normed, axis=-1, keepdims=True)
    return factor * (grad_normed - first_mean - normed * second_mean)


def exact_gelu(vector):
    return jax.nn.gelu(vector, approximate=False)


TILE = 256
NEG = -1e30


def nt_dot(a, b):
    return lax.dot_general(a, b, (((1,), (1,)), ((), ())), preferred_element_type=jnp.float32)


def nn_dot(a, b):
    return lax.dot_general(a, b, (((1,), (0,)), ((), ())), preferred_element_type=jnp.float32)


def tn_dot(a, b):
    return lax.dot_general(a, b, (((0,), (0,)), ((), ())), preferred_element_type=jnp.float32)


def swap_halves(u):
    half = u.shape[-1] // 2
    return jnp.concatenate([u[:, half:], u[:, :half]], axis=1)


def twice(a):
    return jnp.concatenate([a, a], axis=1)


def lane_fold(op, a):
    return op(a[:, : TILE // 2], a[:, TILE // 2 :])


def whole(shape):
    return pl.BlockSpec(shape, lambda *_: (0,) * len(shape))


def project_heads(h_one, weight, cos_tab, sin_tab, heads):
    tok_count, width = h_one.shape
    cols = heads * HD
    rows = 2 * TILE

    def body(h_ref, w_ref, c_ref, s_ref, q_ref, k_ref, v_ref):
        full = nn_dot(h_ref[...], w_ref[...])
        cosine, sine = c_ref[...], s_ref[...]
        for h in range(heads):
            u = full[:, h * HD : (h + 1) * HD]
            turned = (u * cosine + swap_halves(u) * sine).astype(jnp.bfloat16)
            q_ref[h] = (turned.astype(jnp.float32) * HD**-0.5).astype(jnp.bfloat16)
            u = full[:, cols + h * HD : cols + (h + 1) * HD]
            k_ref[h] = (u * cosine + swap_halves(u) * sine).astype(jnp.bfloat16)
            v_ref[h] = full[:, 2 * cols + h * HD : 2 * cols + (h + 1) * HD].astype(jnp.bfloat16)

    out = jax.ShapeDtypeStruct((heads, tok_count, HD), jnp.bfloat16)
    return pl.pallas_call(
        body,
        grid=(tok_count // rows,),
        in_specs=[
            pl.BlockSpec((rows, width), lambda i: (i, 0)),
            whole(weight.shape),
            pl.BlockSpec((rows, HD), lambda i: (i, 0)),
            pl.BlockSpec((rows, HD), lambda i: (i, 0)),
        ],
        out_specs=[pl.BlockSpec((heads, rows, HD), lambda i: (0, i, 0))] * 3,
        out_shape=[out] * 3,
        name="project_heads",
    )(h_one, weight, cos_tab, sin_tab)


def attend(first, last, query, key, value, seg_col, seg_row):
    heads, tok_count, _ = query.shape
    blocks = tok_count // TILE
    half = TILE // 2

    def body(
        first_ref, last_ref, q_ref, k_ref, v_ref, col_ref, row_ref, low_ref, out_ref, lse_ref,
        scores, peak, total, accum,
    ):
        i = pl.program_id(0)
        lo, hi = first_ref[i], last_ref[i]
        peak[...] = jnp.full(peak.shape, NEG, jnp.float32)
        total[...] = jnp.zeros(total.shape, jnp.float32)
        accum[...] = jnp.zeros(accum.shape, jnp.float32)

        def score(j, carry):
            at = pl.multiple_of(j * TILE, TILE)
            same = twice(col_ref[...]) == row_ref[:, pl.ds(at, TILE)]
            for h in range(heads):
                s = jnp.where(same, nt_dot(q_ref[h], k_ref[h, pl.ds(at, TILE), :]), NEG)
                scores[h, j] = s
                peak[h] = jnp.maximum(peak[h], lane_fold(jnp.maximum, s))
            return carry

        lax.fori_loop(lo, hi, score, 0)
        for h in range(heads):
            peak[h] = jnp.broadcast_to(jnp.max(peak[h], axis=1, keepdims=True), (TILE, half))

        def spread(j, carry):
            at = pl.multiple_of(j * TILE, TILE)
            for h in range(heads):
                p = jnp.exp(scores[h, j] - twice(peak[h]))
                total[h] = total[h] + lane_fold(jnp.add, p)
                accum[h] = accum[h] + nn_dot(p.astype(jnp.bfloat16), v_ref[h, pl.ds(at, TILE), :])
            return carry

        lax.fori_loop(lo, hi, spread, 0)
        for h in range(heads):
            norm = jnp.sum(total[h], axis=1, keepdims=True)
            out = accum[h] / norm
            out_ref[h] = out
            low_ref[:, h * HD : (h + 1) * HD] = out.astype(jnp.bfloat16)
            logs = peak[h] + jnp.log(jnp.broadcast_to(norm, (TILE, half)))
            lse_ref[h] = jnp.transpose(logs)[0:1, :]

    tile = pl.BlockSpec((heads, TILE, HD), lambda i, *_: (0, i, 0))
    return pl.pallas_call(
        body,
        grid_spec=pltpu.PrefetchScalarGridSpec(
            num_scalar_prefetch=2,
            grid=(blocks,),
            in_specs=[
                tile,
                whole(key.shape),
                whole(value.shape),
                pl.BlockSpec((TILE, half), lambda i, *_: (i, 0)),
                whole(seg_row.shape),
            ],
            out_specs=[
                pl.BlockSpec((TILE, heads * HD), lambda i, *_: (i, 0)),
                tile,
                pl.BlockSpec((heads, 1, TILE), lambda i, *_: (0, 0, i)),
            ],
            scratch_shapes=[
                pltpu.VMEM((heads, blocks, TILE, TILE), jnp.float32),
                pltpu.VMEM((heads, TILE, half), jnp.float32),
                pltpu.VMEM((heads, TILE, half), jnp.float32),
                pltpu.VMEM((heads, TILE, HD), jnp.float32),
            ],
        ),
        out_shape=[
            jax.ShapeDtypeStruct((tok_count, heads * HD), jnp.bfloat16),
            jax.ShapeDtypeStruct((heads, tok_count, HD), jnp.float32),
            jax.ShapeDtypeStruct((heads, 1, tok_count), jnp.float32),
        ],
        name="attend",
    )(first, last, query, key, value, seg_col, seg_row)


def attend_grad(
    first, last, query, key, value, seg_col, seg_row, grad, out, lse, cos_tab, sin_tab
):
    heads, tok_count, _ = query.shape
    blocks = tok_count // TILE
    half = TILE // 2
    cols = heads * HD

    def body(
        first_ref, last_ref, q_ref, k_ref, v_ref, col_ref, row_ref, g_ref, o_ref, lse_ref,
        c_ref, s_ref, d_ref, split, inner, dq, dk, dv,
    ):
        j = pl.program_id(0)
        lo, hi = first_ref[j], last_ref[j]
        here = pl.ds(pl.multiple_of(j * TILE, TILE), TILE)

        @pl.when(j == 0)
        def _():
            dq[...] = jnp.zeros(dq.shape, jnp.float32)
            for b in range(blocks):
                rows = slice(b * TILE, (b + 1) * TILE)
                for h in range(heads):
                    g = g_ref[rows, h * HD : (h + 1) * HD]
                    split[h, rows, :] = g
                    dots = jnp.sum(g.astype(jnp.float32) * o_ref[h, rows, :], axis=1, keepdims=True)
                    dots = jnp.transpose(jnp.broadcast_to(dots, (TILE, half)))
                    inner[h, :, rows] = dots[0:1, :]

        dk[...] = jnp.zeros(dk.shape, jnp.float32)
        dv[...] = jnp.zeros(dv.shape, jnp.float32)

        def step(i, carry):
            at = pl.ds(pl.multiple_of(i * TILE, TILE), TILE)
            same = twice(col_ref[...]) == row_ref[:, at]
            for h in range(heads):
                q, g, k = q_ref[h, at, :], split[h, at, :], k_ref[h, here, :]
                s = jnp.where(same, nt_dot(k, q), NEG)
                p = jnp.exp(s - lse_ref[h, :, at])
                dp = nt_dot(v_ref[h, here, :], g)
                ds = (p * (dp - inner[h, :, at])).astype(jnp.bfloat16)
                dv[h] = dv[h] + nn_dot(p.astype(jnp.bfloat16), g)
                dk[h] = dk[h] + nn_dot(ds, q)
                dq[h, at, :] = dq[h, at, :] + tn_dot(ds, k)
            return carry

        lax.fori_loop(lo, hi, step, 0)
        cosine, sine = c_ref[here, :], s_ref[here, :]
        for h in range(heads):
            w = dk[h]
            w = (w * cosine - swap_halves(w) * sine).astype(jnp.bfloat16)
            d_ref[here, cols + h * HD : cols + (h + 1) * HD] = w
            d_ref[here, 2 * cols + h * HD : 2 * cols + (h + 1) * HD] = dv[h].astype(jnp.bfloat16)

        @pl.when(j == blocks - 1)
        def _():
            for b in range(blocks):
                rows = slice(b * TILE, (b + 1) * TILE)
                for h in range(heads):
                    w = dq[h, rows, :] * HD**-0.5
                    w = w * c_ref[rows, :] - swap_halves(w) * s_ref[rows, :]
                    d_ref[rows, h * HD : (h + 1) * HD] = w.astype(jnp.bfloat16)

    return pl.pallas_call(
        body,
        grid_spec=pltpu.PrefetchScalarGridSpec(
            num_scalar_prefetch=2,
            grid=(blocks,),
            in_specs=[
                whole(query.shape),
                whole(key.shape),
                whole(value.shape),
                pl.BlockSpec((TILE, half), lambda i, *_: (i, 0)),
                whole(seg_row.shape),
                whole(grad.shape),
                whole(out.shape),
                whole(lse.shape),
                whole(cos_tab.shape),
                whole(sin_tab.shape),
            ],
            out_specs=whole((tok_count, 3 * cols)),
            scratch_shapes=[
                pltpu.VMEM((heads, tok_count, HD), jnp.bfloat16),
                pltpu.VMEM((heads, 1, tok_count), jnp.float32),
                pltpu.VMEM((heads, tok_count, HD), jnp.float32),
                pltpu.VMEM((heads, TILE, HD), jnp.float32),
                pltpu.VMEM((heads, TILE, HD), jnp.float32),
            ],
        ),
        out_shape=jax.ShapeDtypeStruct((tok_count, 3 * cols), jnp.bfloat16),
        name="attend_grad",
    )(first, last, query, key, value, seg_col, seg_row, grad, out, lse, cos_tab, sin_tab)


def shards(
    tokens, lengths, attn_gain, qkv_weight, out_weight, mlp_gain, up_weight, down_weight, cotangent
):
    tok_count = tokens.shape[0]
    qkv_full, up_full = (
        lax.all_gather(qkv_weight, "dp", axis=0, tiled=True),
        lax.all_gather(up_weight, "dp", axis=0, tiled=True),
    )
    out_full, down_full = (
        lax.all_gather(out_weight, "dp", axis=1, tiled=True),
        lax.all_gather(down_weight, "dp", axis=1, tiled=True),
    )
    head_cols = qkv_full.shape[2]
    heads_dev = head_cols // HD
    segment, position = row_layout(lengths[0], tok_count)
    cosine, sine_table = rotary_tables(position, HD)
    source = tokens.astype(jnp.float32)
    normed_one, factor_one = normalize(source)
    h_one = (normed_one * attn_gain).astype(jnp.bfloat16)
    seg_col = jnp.broadcast_to(segment[:, None], (tok_count, TILE // 2))
    seg_row = segment[None, :]
    first, last = tile_ranges(lengths[0], tok_count)
    qkv_flat = qkv_full.reshape(qkv_full.shape[0], 3 * head_cols)
    query, key, value = project_heads(h_one, qkv_flat, cosine, sine_table, heads_dev)
    attended, attended_wide, log_total = attend(first, last, query, key, value, seg_col, seg_row)
    attn_part = jnp.dot(attended, out_full, preferred_element_type=jnp.float32)
    mid = source + lax.psum(attn_part.astype(jnp.bfloat16), "tensor").astype(jnp.float32)
    normed_two, factor_two = normalize(mid)
    h_two = (normed_two * mlp_gain).astype(jnp.bfloat16)
    gate_up = jnp.einsum("td,dcf->tcf", h_two, up_full, preferred_element_type=jnp.float32)
    active, gelu_pull = jax.vjp(exact_gelu, gate_up[:, 0])
    hidden = (active * gate_up[:, 1]).astype(jnp.bfloat16)
    mlp_part = jnp.dot(hidden, down_full, preferred_element_type=jnp.float32)
    output = (mid + lax.psum(mlp_part.astype(jnp.bfloat16), "tensor").astype(jnp.float32)).astype(
        jnp.bfloat16
    )
    grad_down_weight = jnp.einsum(
        "tf,td->fd", hidden, cotangent, preferred_element_type=jnp.float32
    )
    grad_hidden = jnp.einsum(
        "td,fd->tf", cotangent, down_full, preferred_element_type=jnp.float32
    ).astype(jnp.bfloat16)
    grad_wide = grad_hidden.astype(jnp.float32)
    (grad_gate,) = gelu_pull(grad_wide * gate_up[:, 1])
    grad_gate_up = jnp.stack([grad_gate, grad_wide * active], axis=1).astype(jnp.bfloat16)
    grad_up_weight = jnp.einsum(
        "td,tcf->dcf", h_two, grad_gate_up, preferred_element_type=jnp.float32
    )
    grad_h_two = lax.psum(
        jnp.einsum("tcf,dcf->td", grad_gate_up, up_full, preferred_element_type=jnp.float32).astype(
            jnp.bfloat16
        ),
        "tensor",
    ).astype(jnp.float32)
    grad_mlp_gain = jnp.sum(grad_h_two * normed_two, axis=0)
    grad_mid = cotangent.astype(jnp.float32) + norm_back(
        grad_h_two, normed_two, factor_two, mlp_gain
    )
    grad_mid_low = grad_mid.astype(jnp.bfloat16)
    grad_out_weight = jnp.einsum(
        "tf,td->fd", attended, grad_mid_low, preferred_element_type=jnp.float32
    )
    grad_attended = jnp.einsum(
        "td,fd->tf", grad_mid_low, out_full, preferred_element_type=jnp.float32
    ).astype(jnp.bfloat16)
    grad_qkv = attend_grad(
        first,
        last,
        query,
        key,
        value,
        seg_col,
        seg_row,
        grad_attended,
        attended_wide,
        log_total,
        cosine,
        sine_table,
    )
    grad_qkv_weight = jnp.einsum(
        "td,tf->df", h_one, grad_qkv, preferred_element_type=jnp.float32
    ).reshape(-1, 3, head_cols)
    grad_h_one = lax.psum(
        jnp.einsum("tf,df->td", grad_qkv, qkv_flat, preferred_element_type=jnp.float32).astype(
            jnp.bfloat16
        ),
        "tensor",
    ).astype(jnp.float32)
    grad_attn_gain = jnp.sum(grad_h_one * normed_one, axis=0)
    grad_tokens = grad_mid + norm_back(grad_h_one, normed_one, factor_one, attn_gain)
    rows_part = in_one_piece(
        (
            grad_qkv_weight.astype(jnp.bfloat16),
            grad_up_weight.astype(jnp.bfloat16),
            grad_attn_gain.astype(jnp.bfloat16),
            grad_mlp_gain.astype(jnp.bfloat16),
        ),
        "dp",
        0,
        1,
    )
    cols_part = in_one_piece_2(
        (grad_out_weight.astype(jnp.bfloat16), grad_down_weight.astype(jnp.bfloat16)), "dp", 1, 0
    )
    return (
        output,
        grad_tokens,
        rows_part[2],
        rows_part[0],
        cols_part[0],
        rows_part[3],
        rows_part[1],
        cols_part[1],
    )


def solution(mesh):
    in_specs = (
        P("dp", None),
        P("dp", None),
        P(),
        P("dp", None, "tensor"),
        P("tensor", "dp"),
        P(),
        P("dp", None, "tensor"),
        P("tensor", "dp"),
        P("dp", None),
    )
    out_specs = (
        P("dp", None),
        P("dp", None),
        P("dp"),
        P("dp", None, "tensor"),
        P("tensor", "dp"),
        P("dp"),
        P("dp", None, "tensor"),
        P("tensor", "dp"),
    )
    return jax.shard_map(shards, mesh=mesh, in_specs=in_specs, out_specs=out_specs, check_vma=False)
```

```python
import math

import jax
import jax.numpy as jnp
from jax import lax
from jax.experimental import pallas as pl
from jax.experimental.pallas import tpu as pltpu
from jax.sharding import PartitionSpec as P

HD = 64

eps_norm = 1e-05
theta_base = 160000.0


def row_layout(row_lengths, tok_count):
    doc_ends = jnp.cumsum(row_lengths, dtype=jnp.int32)
    tok_place = jnp.arange(tok_count, dtype=jnp.int32)
    passed = tok_place[:, None] >= doc_ends[None, :]
    segment = jnp.sum(passed.astype(jnp.int32), axis=1, dtype=jnp.int32)
    doc_start = jnp.sum(jnp.where(passed, row_lengths[None, :], 0), axis=1, dtype=jnp.int32)
    return (segment, tok_place - doc_start)


def tile_ranges(row_lengths, tok_count):
    ends = jnp.cumsum(row_lengths, dtype=jnp.int32)
    starts = ends - row_lengths
    begin = jnp.arange(tok_count // TILE, dtype=jnp.int32)[:, None] * TILE
    touched = (ends[None, :] > begin) & (starts[None, :] < begin + TILE)
    low = jnp.min(jnp.where(touched, starts[None, :], tok_count), axis=1)
    high = jnp.max(jnp.where(touched, ends[None, :], 0), axis=1)
    return (low // TILE, (high + TILE - 1) // TILE)


def rotary_tables(position, head_width):
    half_width = head_width // 2
    freq_index = jnp.arange(half_width, dtype=jnp.float32)
    inv_freq = jnp.exp(freq_index * (-2.0 * math.log(theta_base) / head_width))
    angles = position.astype(jnp.float32)[:, None] * inv_freq[None, :]
    cosine, sine = jnp.cos(angles), jnp.sin(angles)
    return (jnp.concatenate([cosine, cosine], axis=1), jnp.concatenate([-sine, sine], axis=1))


def normalize(vector):
    row_mean = jnp.mean(vector, axis=-1, keepdims=True)
    centred = vector - row_mean
    spread = jnp.mean(centred * centred, axis=-1, keepdims=True)
    factor = lax.rsqrt(spread + eps_norm)
    return (centred * factor, factor)


def norm_back(grad_norm_out, normed, factor, gain_vec):
    grad_normed = grad_norm_out * gain_vec
    first_mean = jnp.mean(grad_normed, axis=-1, keepdims=True)
    second_mean = jnp.mean(grad_normed * normed, axis=-1, keepdims=True)
    return factor * (grad_normed - first_mean - normed * second_mean)


TILE = 256
NEG = -1e30


def nt_dot(a, b):
    return lax.dot_general(a, b, (((1,), (1,)), ((), ())), preferred_element_type=jnp.float32)


def nn_dot(a, b):
    return lax.dot_general(a, b, (((1,), (0,)), ((), ())), preferred_element_type=jnp.float32)


def tn_dot(a, b):
    return lax.dot_general(a, b, (((0,), (0,)), ((), ())), preferred_element_type=jnp.float32)


def swap_halves(u):
    half = u.shape[-1] // 2
    return jnp.concatenate([u[:, half:], u[:, :half]], axis=1)


def twice(a):
    return jnp.concatenate([a, a], axis=1)


def lane_fold(op, a):
    return op(a[:, : TILE // 2], a[:, TILE // 2 :])


def whole(shape):
    return pl.BlockSpec(shape, lambda *_: (0,) * len(shape))


def project_heads(h_one, weight, cos_tab, sin_tab, heads):
    tok_count, width = h_one.shape
    cols = heads * HD
    rows = 2 * TILE

    def body(h_ref, w_ref, c_ref, s_ref, q_ref, k_ref, v_ref):
        full = nn_dot(h_ref[...], w_ref[...])
        cosine, sine = c_ref[...], s_ref[...]
        for h in range(heads):
            u = full[:, h * HD : (h + 1) * HD]
            turned = (u * cosine + swap_halves(u) * sine).astype(jnp.bfloat16)
            q_ref[h] = (turned.astype(jnp.float32) * HD**-0.5).astype(jnp.bfloat16)
            u = full[:, cols + h * HD : cols + (h + 1) * HD]
            k_ref[h] = (u * cosine + swap_halves(u) * sine).astype(jnp.bfloat16)
            v_ref[h] = full[:, 2 * cols + h * HD : 2 * cols + (h + 1) * HD].astype(jnp.bfloat16)

    out = jax.ShapeDtypeStruct((heads, tok_count, HD), jnp.bfloat16)
    return pl.pallas_call(
        body,
        grid=(tok_count // rows,),
        in_specs=[
            pl.BlockSpec((rows, width), lambda i: (i, 0)),
            whole(weight.shape),
            pl.BlockSpec((rows, HD), lambda i: (i, 0)),
            pl.BlockSpec((rows, HD), lambda i: (i, 0)),
        ],
        out_specs=[pl.BlockSpec((heads, rows, HD), lambda i: (0, i, 0))] * 3,
        out_shape=[out] * 3,
        name="project_heads",
    )(h_one, weight, cos_tab, sin_tab)


def attend(first, last, place, query, key, value, seg_col, seg_row, parts):
    heads, tok_count, _ = query.shape
    blocks = tok_count // TILE
    share = blocks // parts
    half = TILE // 2

    def body(
        first_ref, last_ref, place_ref, q_ref, k_ref, v_ref, col_ref, row_ref, *refs
    ):
        low_refs, (out_ref, lse_ref, scores, peak, total, accum, low) = refs[:parts], refs[parts:]
        i = pl.program_id(0)
        lo, hi = first_ref[i], last_ref[i]
        peak[...] = jnp.full(peak.shape, NEG, jnp.float32)
        total[...] = jnp.zeros(total.shape, jnp.float32)
        accum[...] = jnp.zeros(accum.shape, jnp.float32)

        def score(j, carry):
            at = pl.multiple_of(j * TILE, TILE)
            same = twice(col_ref[...]) == row_ref[:, pl.ds(at, TILE)]
            for h in range(heads):
                s = jnp.where(same, nt_dot(q_ref[h], k_ref[h, pl.ds(at, TILE), :]), NEG)
                scores[h, j] = s
                peak[h] = jnp.maximum(peak[h], lane_fold(jnp.maximum, s))
            return carry

        lax.fori_loop(lo, hi, score, 0)
        for h in range(heads):
            peak[h] = jnp.broadcast_to(jnp.max(peak[h], axis=1, keepdims=True), (TILE, half))

        def spread(j, carry):
            at = pl.multiple_of(j * TILE, TILE)
            for h in range(heads):
                p = jnp.exp(scores[h, j] - twice(peak[h]))
                total[h] = total[h] + lane_fold(jnp.add, p)
                accum[h] = accum[h] + nn_dot(p.astype(jnp.bfloat16), v_ref[h, pl.ds(at, TILE), :])
            return carry

        lax.fori_loop(lo, hi, spread, 0)
        for h in range(heads):
            norm = jnp.sum(total[h], axis=1, keepdims=True)
            out = accum[h] / norm
            out_ref[h] = out
            low[:, h * HD : (h + 1) * HD] = out.astype(jnp.bfloat16)
            logs = peak[h] + jnp.log(jnp.broadcast_to(norm, (TILE, half)))
            lse_ref[h] = jnp.transpose(logs)[0:1, :]
        rows = pl.ds(pl.multiple_of((i % share) * TILE, TILE), TILE)
        for r in range(parts):

            @pl.when((i // share) ^ place_ref[0] == r)
            def _():
                low_refs[r][rows, :] = low[...]

    tile = pl.BlockSpec((heads, TILE, HD), lambda i, *_: (0, i, 0))
    return pl.pallas_call(
        body,
        grid_spec=pltpu.PrefetchScalarGridSpec(
            num_scalar_prefetch=3,
            grid=(blocks,),
            in_specs=[
                tile,
                whole(key.shape),
                whole(value.shape),
                pl.BlockSpec((TILE, half), lambda i, *_: (i, 0)),
                whole(seg_row.shape),
            ],
            out_specs=[whole((share * TILE, heads * HD))] * parts
            + [
                tile,
                pl.BlockSpec((heads, 1, TILE), lambda i, *_: (0, 0, i)),
            ],
            scratch_shapes=[
                pltpu.VMEM((heads, blocks, TILE, TILE), jnp.float32),
                pltpu.VMEM((heads, TILE, half), jnp.float32),
                pltpu.VMEM((heads, TILE, half), jnp.float32),
                pltpu.VMEM((heads, TILE, HD), jnp.float32),
                pltpu.VMEM((TILE, heads * HD), jnp.bfloat16),
            ],
        ),
        out_shape=[jax.ShapeDtypeStruct((share * TILE, heads * HD), jnp.bfloat16)] * parts
        + [
            jax.ShapeDtypeStruct((heads, tok_count, HD), jnp.float32),
            jax.ShapeDtypeStruct((heads, 1, tok_count), jnp.float32),
        ],
        name="attend",
    )(first, last, place, query, key, value, seg_col, seg_row)


def attend_grad(
    first, last, place, query, key, value, seg_col, seg_row, grads, out, lse, cos_tab, sin_tab
):
    heads, tok_count, _ = query.shape
    blocks = tok_count // TILE
    half = TILE // 2
    cols = heads * HD
    parts = len(grads)
    share = tok_count // parts

    def body(
        first_ref, last_ref, place_ref, q_ref, k_ref, v_ref, col_ref, row_ref, o_ref, lse_ref,
        c_ref, s_ref, *refs
    ):
        g_refs, (d_ref, split, inner, dq, dk, dv) = refs[:parts], refs[parts:]
        j = pl.program_id(0)
        lo, hi = first_ref[j], last_ref[j]
        here = pl.ds(pl.multiple_of(j * TILE, TILE), TILE)

        @pl.when(j == 0)
        def _():
            dq[...] = jnp.zeros(dq.shape, jnp.float32)
            for b in range(blocks):
                r, off = b * TILE // share, b * TILE % share
                base = (place_ref[0] ^ r) * share + off
                rows = pl.ds(pl.multiple_of(base, TILE), TILE)
                for h in range(heads):
                    g = g_refs[r][off : off + TILE, h * HD : (h + 1) * HD]
                    split[h, rows, :] = g
                    dots = jnp.sum(g.astype(jnp.float32) * o_ref[h, rows, :], axis=1, keepdims=True)
                    dots = jnp.transpose(jnp.broadcast_to(dots, (TILE, half)))
                    inner[h, :, rows] = dots[0:1, :]

        dk[...] = jnp.zeros(dk.shape, jnp.float32)
        dv[...] = jnp.zeros(dv.shape, jnp.float32)

        def step(i, carry):
            at = pl.ds(pl.multiple_of(i * TILE, TILE), TILE)
            same = twice(col_ref[...]) == row_ref[:, at]
            for h in range(heads):
                q, g, k = q_ref[h, at, :], split[h, at, :], k_ref[h, here, :]
                s = jnp.where(same, nt_dot(k, q), NEG)
                p = jnp.exp(s - lse_ref[h, :, at])
                dp = nt_dot(v_ref[h, here, :], g)
                ds = (p * (dp - inner[h, :, at])).astype(jnp.bfloat16)
                dv[h] = dv[h] + nn_dot(p.astype(jnp.bfloat16), g)
                dk[h] = dk[h] + nn_dot(ds, q)
                dq[h, at, :] = dq[h, at, :] + tn_dot(ds, k)
            return carry

        lax.fori_loop(lo, hi, step, 0)
        cosine, sine = c_ref[here, :], s_ref[here, :]
        for h in range(heads):
            w = dk[h]
            w = (w * cosine - swap_halves(w) * sine).astype(jnp.bfloat16)
            d_ref[here, cols + h * HD : cols + (h + 1) * HD] = w
            d_ref[here, 2 * cols + h * HD : 2 * cols + (h + 1) * HD] = dv[h].astype(jnp.bfloat16)

        @pl.when(j == blocks - 1)
        def _():
            for b in range(blocks):
                rows = slice(b * TILE, (b + 1) * TILE)
                for h in range(heads):
                    w = dq[h, rows, :] * HD**-0.5
                    w = w * c_ref[rows, :] - swap_halves(w) * s_ref[rows, :]
                    d_ref[rows, h * HD : (h + 1) * HD] = w.astype(jnp.bfloat16)

    return pl.pallas_call(
        body,
        grid_spec=pltpu.PrefetchScalarGridSpec(
            num_scalar_prefetch=3,
            grid=(blocks,),
            in_specs=[
                whole(query.shape),
                whole(key.shape),
                whole(value.shape),
                pl.BlockSpec((TILE, half), lambda i, *_: (i, 0)),
                whole(seg_row.shape),
                whole(out.shape),
                whole(lse.shape),
                whole(cos_tab.shape),
                whole(sin_tab.shape),
            ]
            + [whole(g.shape) for g in grads],
            out_specs=whole((tok_count, 3 * cols)),
            scratch_shapes=[
                pltpu.VMEM((heads, tok_count, HD), jnp.bfloat16),
                pltpu.VMEM((heads, 1, tok_count), jnp.float32),
                pltpu.VMEM((heads, tok_count, HD), jnp.float32),
                pltpu.VMEM((heads, TILE, HD), jnp.float32),
                pltpu.VMEM((heads, TILE, HD), jnp.float32),
            ],
        ),
        out_shape=jax.ShapeDtypeStruct((tok_count, 3 * cols), jnp.bfloat16),
        name="attend_grad",
    )(first, last, place, query, key, value, seg_col, seg_row, out, lse, cos_tab, sin_tab, *grads)


def swap(value, axis, step):
    count = lax.axis_size(axis)
    return lax.ppermute(value, axis, [(i, i ^ step) for i in range(count)])


def gather_pieces(shard):
    pieces = {0: shard}
    count = lax.axis_size("dp")
    for step in range(2, count, 2):
        pieces[step] = swap(shard, "dp", step)
    for step in range(0, count, 2):
        pieces[step + 1] = swap(pieces[step], "dp", 1)
    return [pieces[r] for r in range(count)]


def assemble(pieces, place):
    count = len(pieces)
    lead, (rows, cols) = pieces[0].shape[:-2], pieces[0].shape[-2:]
    if rows % 16:
        order = place[0] ^ jnp.arange(count, dtype=jnp.int32)
        ranked = jnp.take(jnp.stack(pieces), order, axis=0)
        return jnp.moveaxis(ranked, 0, -3).reshape(*lead, count * rows, cols)

    def body(place_ref, *refs):
        out_ref, sems = refs[count], refs[count + 1]
        copies = []
        for r in range(count):
            at = pl.ds(pl.multiple_of((place_ref[0] ^ r) * rows, 16), rows)
            target = out_ref.at[(slice(None),) * len(lead) + (at,)]
            copies.append(pltpu.make_async_copy(refs[r], target, sems.at[r]))
        for copy in copies:
            copy.start()
        for copy in copies:
            copy.wait()

    return pl.pallas_call(
        body,
        grid_spec=pltpu.PrefetchScalarGridSpec(
            num_scalar_prefetch=1,
            grid=(1,),
            in_specs=[pl.BlockSpec(memory_space=pl.ANY)] * count,
            out_specs=pl.BlockSpec(memory_space=pl.ANY),
            scratch_shapes=[pltpu.SemaphoreType.DMA((count,))],
        ),
        out_shape=jax.ShapeDtypeStruct((*lead, count * rows, cols), pieces[0].dtype),
        name="assemble",
    )(place, *pieces)


def reduce_pieces(total, place):
    count = lax.axis_size("dp")
    rows, cols = total.shape[0] // count, total.shape[1]
    order = place[0] ^ jnp.array([*range(0, count, 2), *range(1, count, 2)], jnp.int32)
    ranked = jnp.take(total.reshape(count, rows, cols), order, axis=0)
    near, far = ranked[: count // 2], ranked[count // 2 :]
    near = near.astype(jnp.float32) + swap(far, "dp", 1).astype(jnp.float32)
    low = near.astype(jnp.bfloat16)
    result = near[0]
    for slot in range(1, count // 2):
        result = result + swap(low[slot], "dp", 2 * slot).astype(jnp.float32)
    return result


def layer(
    att, source, cot, gain, weight_near, weight_far, hid
):
    tok_count, width = source.shape
    head_cols = att[0].shape[1]
    parts = len(att)
    ff = parts * hid
    inner = parts * head_cols
    rows = 256

    def body(*refs):
        a_refs = refs[:parts]
        x_ref, c_ref, g_ref, wa_ref, wb_ref = refs[parts : parts + 5]
        out_ref, dmid_ref, dlow_ref, h_ref, hid_ref, dg_ref, dv_ref, gg_ref = refs[
            parts + 5 : parts + 13
        ]
        d_refs = refs[parts + 13 : 2 * parts + 13]
        gate, lift, down, proj = refs[2 * parts + 13 :]

        @pl.when(pl.program_id(0) == 0)
        def _():
            gg_ref[...] = jnp.zeros(gg_ref.shape, jnp.float32)
            for slot in range(parts):
                w_ref, s = (wa_ref, wb_ref)[slot // 2], slot % 2
                at = slice(slot * hid, (slot + 1) * hid)
                gate[:, at] = w_ref[s, :, :hid]
                lift[:, at] = w_ref[s, :, hid : 2 * hid]
                down[:, at] = w_ref[s, :, 2 * hid : 3 * hid]
                proj[:, slot * head_cols : (slot + 1) * head_cols] = w_ref[
                    s, :, 3 * hid : 3 * hid + head_cols
                ]

        gain_vec = g_ref[...]
        attended = jnp.concatenate([a_refs[r][...] for r in SLOTS], axis=1)
        mid = x_ref[...].astype(jnp.float32) + nt_dot(attended, proj[...])
        normed, factor = normalize(mid)
        h_two = (normed * gain_vec).astype(jnp.bfloat16)
        h_ref[...] = h_two
        cot_low = c_ref[...]
        first = nn_dot(h_two, gate[...])
        second = nn_dot(h_two, lift[...])
        below = 0.5 * (1.0 + lax.erf(first * math.sqrt(0.5)))
        active = first * below
        hidden = (active * second).astype(jnp.bfloat16)
        hid_ref[...] = hidden
        out_ref[...] = (mid + nt_dot(hidden, down[...])).astype(jnp.bfloat16)
        slope = below + first * (jnp.exp(-0.5 * first * first) * (1.0 / math.sqrt(2.0 * math.pi)))
        d_hidden = nn_dot(cot_low, down[...]).astype(jnp.bfloat16).astype(jnp.float32)
        d_first = (d_hidden * second * slope).astype(jnp.bfloat16)
        d_second = (d_hidden * active).astype(jnp.bfloat16)
        dg_ref[...] = d_first
        dv_ref[...] = d_second
        d_h = nt_dot(d_first, gate[...]) + nt_dot(d_second, lift[...])
        gg_ref[...] += jnp.sum(d_h * normed, axis=0, keepdims=True)
        d_mid = cot_low.astype(jnp.float32) + norm_back(d_h, normed, factor, gain_vec)
        dmid_ref[...] = d_mid
        d_low = d_mid.astype(jnp.bfloat16)
        dlow_ref[...] = d_low
        d_att = nn_dot(d_low, proj[...]).astype(jnp.bfloat16)
        for slot in range(parts):
            d_refs[SLOTS[slot]][...] = d_att[:, slot * head_cols : (slot + 1) * head_cols]

    def tile(cols):
        return pl.BlockSpec((rows, cols), lambda i: (i, 0))

    def fixed(shape):
        return pl.BlockSpec(shape, lambda *_: (0,) * len(shape), pipeline_mode=pl.Buffered(1))

    def shape(cols, kind=jnp.bfloat16):
        return jax.ShapeDtypeStruct((tok_count, cols), kind)

    return pl.pallas_call(
        body,
        grid=(tok_count // rows,),
        in_specs=[tile(head_cols)] * parts
        + [tile(width), tile(width), whole((1, width))]
        + [fixed(weight_near.shape), fixed(weight_far.shape)],
        out_specs=[tile(width)] * 4
        + [tile(ff)] * 3
        + [whole((1, width))]
        + [tile(head_cols)] * parts,
        out_shape=[
            shape(width),
            shape(width, jnp.float32),
            shape(width),
            shape(width),
            shape(ff),
            shape(ff),
            shape(ff),
            jax.ShapeDtypeStruct((1, width), jnp.float32),
        ]
        + [shape(head_cols)] * parts,
        scratch_shapes=[
            pltpu.VMEM((width, ff), jnp.bfloat16),
            pltpu.VMEM((width, ff), jnp.bfloat16),
            pltpu.VMEM((width, ff), jnp.bfloat16),
            pltpu.VMEM((width, inner), jnp.bfloat16),
        ],
        name="layer",
    )(*att, source, cot, gain[None, :], weight_near, weight_far)


SLOTS = (0, 2, 1, 3)


def weight_grads(side, h_two, d_first, d_second, cot, hidden, d_low, att, gain_grad, wide):
    tok_count, width = h_two.shape
    hid = hidden.shape[1] // len(SLOTS)
    head_cols = att[0].shape[1]
    both = tuple(att[r] for r in SLOTS[2 * side : 2 * side + 2])
    here = slice(2 * side * hid, (2 * side + 2) * hid)

    def body(h_ref, f_ref, s_ref, c_ref, u_ref, l_ref, a_ref, b_ref, g_ref, out_ref):
        for ref, turned, at in ((f_ref, h_ref, 0), (s_ref, h_ref, hid), (u_ref, c_ref, 2 * hid)):
            full = tn_dot(turned[...], ref[:, here]).astype(jnp.bfloat16)
            out_ref[0, :, at : at + hid] = full[:, :hid]
            out_ref[1, :, at : at + hid] = full[:, hid:]
        gain_col = jnp.transpose(jnp.broadcast_to(g_ref[...], (128, width))).astype(jnp.bfloat16)
        for s, ref in ((0, a_ref), (1, b_ref)):
            at = 3 * hid
            out_ref[s, :, at : at + head_cols] = tn_dot(l_ref[...], ref[...]).astype(jnp.bfloat16)
            out_ref[s, :, at + head_cols :] = gain_col[:, : wide - at - head_cols]

    return pl.pallas_call(
        body,
        out_shape=jax.ShapeDtypeStruct((2, width, wide), jnp.bfloat16),
        name="weight_grads",
    )(h_two, d_first, d_second, cot, hidden, d_low, *both, gain_grad)


def back_to_width(d_qkv, weight, place, slots, share):
    width, cols = weight.shape
    first, stride = slots[0], slots[1] - slots[0]

    def body(place_ref, d_ref, w_ref, out_ref):
        out_ref[0] = nt_dot(d_ref[...], w_ref[...]).astype(jnp.bfloat16)

    return pl.pallas_call(
        body,
        grid_spec=pltpu.PrefetchScalarGridSpec(
            num_scalar_prefetch=1,
            grid=(len(slots),),
            in_specs=[
                pl.BlockSpec((share, cols), lambda i, at: (at[0] ^ (first + stride * i), 0)),
                whole(weight.shape),
            ],
            out_specs=pl.BlockSpec((1, share, width), lambda i, at: (i, 0, 0)),
        ),
        out_shape=jax.ShapeDtypeStruct((len(slots), share, width), jnp.bfloat16),
        name="back_to_width",
    )(place, d_qkv, weight)


def share_rows(mine, place):
    other = swap(mine, "tensor", 2)
    far = swap(jnp.stack([mine, other]), "tensor", 1)
    return assemble([mine, far[0], other, far[1]], place)


def shards(
    tokens, lengths, attn_gain, qkv_weight, out_weight, mlp_gain, up_weight, down_weight, cotangent
):
    tok_count, width = tokens.shape
    parts = lax.axis_size("tensor")
    share = tok_count // parts
    rank = lax.axis_index("tensor").astype(jnp.int32)
    place = rank[None]
    dp_place = lax.axis_index("dp").astype(jnp.int32)[None]
    rows = qkv_weight.shape[0]
    head_cols = qkv_weight.shape[2]
    heads_dev = head_cols // HD
    hid = up_weight.shape[2]
    used = 3 * hid + head_cols
    wide = used // 128 * 128 + 128

    qkv_flat = assemble(gather_pieces(qkv_weight.reshape(rows, 3 * head_cols)), dp_place)
    packed = jnp.concatenate(
        [
            up_weight.reshape(rows, 2 * hid),
            down_weight.T,
            out_weight.T,
            jnp.zeros((rows, wide - used), jnp.bfloat16),
        ],
        axis=1,
    )
    paired = jnp.stack([packed, swap(packed, "tensor", 2)])
    weight_near = assemble(gather_pieces(paired), dp_place)
    weight_far = swap(weight_near, "tensor", 1)

    segment, position = row_layout(lengths[0], tok_count)
    cosine, sine_table = rotary_tables(position, HD)
    h_one = (normalize(tokens.astype(jnp.float32))[0] * attn_gain).astype(jnp.bfloat16)
    seg_col = jnp.broadcast_to(segment[:, None], (tok_count, TILE // 2))
    seg_row = segment[None, :]
    first, last = tile_ranges(lengths[0], tok_count)
    query, key, value = project_heads(h_one, qkv_flat, cosine, sine_table, heads_dev)
    *sent, attended_wide, log_total = attend(
        first, last, place, query, key, value, seg_col, seg_row, parts
    )
    att = [sent[0]] + [swap(sent[r], "tensor", r) for r in range(1, parts)]
    my_tokens = lax.dynamic_slice_in_dim(tokens, rank * share, share, 0)
    my_cot = lax.dynamic_slice_in_dim(cotangent, rank * share, share, 0)
    out, d_mid, d_low, h_two, hidden, d_first, d_second, gain_two, *d_sent = layer(
        att, my_tokens, my_cot, mlp_gain, weight_near, weight_far, hid
    )
    d_att = [d_sent[0]] + [swap(d_sent[r], "tensor", r) for r in range(1, parts)]
    output = share_rows(out, place)

    grads_in = (h_two, d_first, d_second, my_cot, hidden, d_low, att, gain_two, wide)
    grads_far = weight_grads(1, *grads_in)
    grads_near = weight_grads(0, *grads_in)
    chip = grads_near.astype(jnp.float32) + swap(grads_far, "tensor", 1).astype(jnp.float32)
    column = chip[0] + swap(chip[1].astype(jnp.bfloat16), "tensor", 2).astype(jnp.float32)
    reduced = reduce_pieces(column.astype(jnp.bfloat16), dp_place)
    up_grad = reduced[:, : 2 * hid].reshape(rows, 2, hid)
    down_grad = reduced[:, 2 * hid : 3 * hid].T
    out_grad = reduced[:, 3 * hid : used].T
    mlp_gain_grad = reduced[:, used]

    d_qkv = attend_grad(
        first,
        last,
        place,
        query,
        key,
        value,
        seg_col,
        seg_row,
        d_att,
        attended_wide,
        log_total,
        cosine,
        sine_table,
    )
    d_far = back_to_width(d_qkv, qkv_flat, place, (1, 3), share)
    d_near = back_to_width(d_qkv, qkv_flat, place, (0, 2), share)
    d_chip = d_near.astype(jnp.float32) + swap(d_far, "tensor", 1).astype(jnp.float32)
    d_h_one = d_chip[0] + swap(d_chip[1].astype(jnp.bfloat16), "tensor", 2).astype(jnp.float32)
    normed_one, factor_one = normalize(my_tokens.astype(jnp.float32))
    tokens_grad = d_mid + norm_back(d_h_one, normed_one, factor_one, attn_gain)
    tokens_grad = share_rows(tokens_grad.astype(jnp.bfloat16), place).astype(jnp.float32)
    gain_one = jnp.sum(d_h_one * normed_one, axis=0)[None, :]
    gain_one = gain_one + sum(swap(gain_one, "tensor", r) for r in range(1, parts))
    gain_one = gain_one + sum(swap(gain_one, "dp", r) for r in range(1, lax.axis_size("dp")))
    attn_gain_grad = lax.dynamic_slice_in_dim(gain_one[0], dp_place[0] * rows, rows, 0)
    qkv_total = jnp.einsum("td,tf->df", h_one, d_qkv, preferred_element_type=jnp.float32)
    qkv_grad = reduce_pieces(qkv_total.astype(jnp.bfloat16), dp_place).reshape(rows, 3, head_cols)
    return (
        output,
        tokens_grad,
        attn_gain_grad,
        qkv_grad,
        out_grad,
        mlp_gain_grad,
        up_grad,
        down_grad,
    )


def solution(mesh):
    in_specs = (
        P("dp", None),
        P("dp", None),
        P(),
        P("dp", None, "tensor"),
        P("tensor", "dp"),
        P(),
        P("dp", None, "tensor"),
        P("tensor", "dp"),
        P("dp", None),
    )
    out_specs = (
        P("dp", None),
        P("dp", None),
        P("dp"),
        P("dp", None, "tensor"),
        P("tensor", "dp"),
        P("dp"),
        P("dp", None, "tensor"),
        P("tensor", "dp"),
    )
    return jax.shard_map(shards, mesh=mesh, in_specs=in_specs, out_specs=out_specs, check_vma=False)
```

```python
import math

import jax
import jax.numpy as jnp
from jax import lax
from jax.experimental import pallas as pl
from jax.experimental.pallas import tpu as pltpu
from jax.sharding import PartitionSpec as P

HD = 64

eps_norm = 1e-05
theta_base = 160000.0


def row_layout(row_lengths, tok_count):
    doc_ends = jnp.cumsum(row_lengths, dtype=jnp.int32)
    tok_place = jnp.arange(tok_count, dtype=jnp.int32)
    passed = tok_place[:, None] >= doc_ends[None, :]
    segment = jnp.sum(passed.astype(jnp.int32), axis=1, dtype=jnp.int32)
    doc_start = jnp.sum(jnp.where(passed, row_lengths[None, :], 0), axis=1, dtype=jnp.int32)
    return (segment, tok_place - doc_start)


def tile_ranges(row_lengths, tok_count):
    ends = jnp.cumsum(row_lengths, dtype=jnp.int32)
    starts = ends - row_lengths
    begin = jnp.arange(tok_count // TILE, dtype=jnp.int32)[:, None] * TILE
    touched = (ends[None, :] > begin) & (starts[None, :] < begin + TILE)
    low = jnp.min(jnp.where(touched, starts[None, :], tok_count), axis=1)
    high = jnp.max(jnp.where(touched, ends[None, :], 0), axis=1)
    return (low // TILE, (high + TILE - 1) // TILE)


def rotary_tables(position, head_width):
    half_width = head_width // 2
    freq_index = jnp.arange(half_width, dtype=jnp.float32)
    inv_freq = jnp.exp(freq_index * (-2.0 * math.log(theta_base) / head_width))
    angles = position.astype(jnp.float32)[:, None] * inv_freq[None, :]
    cosine, sine = jnp.cos(angles), jnp.sin(angles)
    return (jnp.concatenate([cosine, cosine], axis=1), jnp.concatenate([-sine, sine], axis=1))


def normalize(vector):
    row_mean = jnp.mean(vector, axis=-1, keepdims=True)
    centred = vector - row_mean
    spread = jnp.mean(centred * centred, axis=-1, keepdims=True)
    factor = lax.rsqrt(spread + eps_norm)
    return (centred * factor, factor)


def norm_back(grad_norm_out, normed, factor, gain_vec):
    grad_normed = grad_norm_out * gain_vec
    first_mean = jnp.mean(grad_normed, axis=-1, keepdims=True)
    second_mean = jnp.mean(grad_normed * normed, axis=-1, keepdims=True)
    return factor * (grad_normed - first_mean - normed * second_mean)


TILE = 256
NEG = -1e30


def nt_dot(a, b):
    return lax.dot_general(a, b, (((1,), (1,)), ((), ())), preferred_element_type=jnp.float32)


def nn_dot(a, b):
    return lax.dot_general(a, b, (((1,), (0,)), ((), ())), preferred_element_type=jnp.float32)


def tn_dot(a, b):
    return lax.dot_general(a, b, (((0,), (0,)), ((), ())), preferred_element_type=jnp.float32)


def swap_halves(u):
    half = u.shape[-1] // 2
    return jnp.concatenate([u[:, half:], u[:, :half]], axis=1)


def twice(a):
    return jnp.concatenate([a, a], axis=1)


def lane_fold(op, a):
    return op(a[:, : TILE // 2], a[:, TILE // 2 :])


def whole(shape):
    return pl.BlockSpec(shape, lambda *_: (0,) * len(shape))


def project_heads(h_one, weight, cos_tab, sin_tab, heads):
    tok_count, width = h_one.shape
    cols = heads * HD
    rows = 2 * TILE

    def body(h_ref, w_ref, c_ref, s_ref, q_ref, k_ref, v_ref):
        full = nn_dot(h_ref[...], w_ref[...])
        cosine, sine = c_ref[...], s_ref[...]
        for h in range(heads):
            u = full[:, h * HD : (h + 1) * HD]
            turned = (u * cosine + swap_halves(u) * sine).astype(jnp.bfloat16)
            q_ref[h] = (turned.astype(jnp.float32) * HD**-0.5).astype(jnp.bfloat16)
            u = full[:, cols + h * HD : cols + (h + 1) * HD]
            k_ref[h] = (u * cosine + swap_halves(u) * sine).astype(jnp.bfloat16)
            v_ref[h] = full[:, 2 * cols + h * HD : 2 * cols + (h + 1) * HD].astype(jnp.bfloat16)

    out = jax.ShapeDtypeStruct((heads, tok_count, HD), jnp.bfloat16)
    return pl.pallas_call(
        body,
        grid=(tok_count // rows,),
        in_specs=[
            pl.BlockSpec((rows, width), lambda i: (i, 0)),
            whole(weight.shape),
            pl.BlockSpec((rows, HD), lambda i: (i, 0)),
            pl.BlockSpec((rows, HD), lambda i: (i, 0)),
        ],
        out_specs=[pl.BlockSpec((heads, rows, HD), lambda i: (0, i, 0))] * 3,
        out_shape=[out] * 3,
        name="project_heads",
    )(h_one, weight, cos_tab, sin_tab)


def attend(first, last, place, query, key, value, seg_col, seg_row, parts):
    heads, tok_count, _ = query.shape
    blocks = tok_count // TILE
    share = blocks // parts
    half = TILE // 2

    def body(
        first_ref, last_ref, place_ref, q_ref, k_ref, v_ref, col_ref, row_ref, *refs
    ):
        low_refs, (out_ref, lse_ref, scores, peak, total, accum, low) = refs[:parts], refs[parts:]
        i = pl.program_id(0)
        lo, hi = first_ref[i], last_ref[i]
        peak[...] = jnp.full(peak.shape, NEG, jnp.float32)
        total[...] = jnp.zeros(total.shape, jnp.float32)
        accum[...] = jnp.zeros(accum.shape, jnp.float32)

        def score(j, carry):
            at = pl.multiple_of(j * TILE, TILE)
            same = twice(col_ref[...]) == row_ref[:, pl.ds(at, TILE)]
            for h in range(heads):
                s = jnp.where(same, nt_dot(q_ref[h], k_ref[h, pl.ds(at, TILE), :]), NEG)
                scores[h, j] = s
                peak[h] = jnp.maximum(peak[h], lane_fold(jnp.maximum, s))
            return carry

        lax.fori_loop(lo, hi, score, 0)
        for h in range(heads):
            peak[h] = jnp.broadcast_to(jnp.max(peak[h], axis=1, keepdims=True), (TILE, half))

        def spread(j, carry):
            at = pl.multiple_of(j * TILE, TILE)
            for h in range(heads):
                p = jnp.exp(scores[h, j] - twice(peak[h]))
                total[h] = total[h] + lane_fold(jnp.add, p)
                accum[h] = accum[h] + nn_dot(p.astype(jnp.bfloat16), v_ref[h, pl.ds(at, TILE), :])
            return carry

        lax.fori_loop(lo, hi, spread, 0)
        for h in range(heads):
            norm = jnp.sum(total[h], axis=1, keepdims=True)
            out = accum[h] / norm
            out_ref[h] = out
            low[:, h * HD : (h + 1) * HD] = out.astype(jnp.bfloat16)
            logs = peak[h] + jnp.log(jnp.broadcast_to(norm, (TILE, half)))
            lse_ref[h] = jnp.transpose(logs)[0:1, :]
        rows = pl.ds(pl.multiple_of((i % share) * TILE, TILE), TILE)
        for r in range(parts):

            @pl.when((i // share) ^ place_ref[0] == r)
            def _():
                low_refs[r][rows, :] = low[...]

    tile = pl.BlockSpec((heads, TILE, HD), lambda i, *_: (0, i, 0))
    return pl.pallas_call(
        body,
        grid_spec=pltpu.PrefetchScalarGridSpec(
            num_scalar_prefetch=3,
            grid=(blocks,),
            in_specs=[
                tile,
                whole(key.shape),
                whole(value.shape),
                pl.BlockSpec((TILE, half), lambda i, *_: (i, 0)),
                whole(seg_row.shape),
            ],
            out_specs=[whole((share * TILE, heads * HD))] * parts
            + [
                tile,
                pl.BlockSpec((heads, 1, TILE), lambda i, *_: (0, 0, i)),
            ],
            scratch_shapes=[
                pltpu.VMEM((heads, blocks, TILE, TILE), jnp.float32),
                pltpu.VMEM((heads, TILE, half), jnp.float32),
                pltpu.VMEM((heads, TILE, half), jnp.float32),
                pltpu.VMEM((heads, TILE, HD), jnp.float32),
                pltpu.VMEM((TILE, heads * HD), jnp.bfloat16),
            ],
        ),
        out_shape=[jax.ShapeDtypeStruct((share * TILE, heads * HD), jnp.bfloat16)] * parts
        + [
            jax.ShapeDtypeStruct((heads, tok_count, HD), jnp.float32),
            jax.ShapeDtypeStruct((heads, 1, tok_count), jnp.float32),
        ],
        name="attend",
    )(first, last, place, query, key, value, seg_col, seg_row)


def attend_grad(
    first, last, place, query, key, value, seg_col, seg_row, grads, out, lse, cos_tab, sin_tab
):
    heads, tok_count, _ = query.shape
    blocks = tok_count // TILE
    half = TILE // 2
    cols = heads * HD
    parts = len(grads)
    share = tok_count // parts

    def body(
        first_ref, last_ref, place_ref, q_ref, k_ref, v_ref, col_ref, row_ref, o_ref, lse_ref,
        c_ref, s_ref, *refs
    ):
        g_refs, (d_ref, split, inner, dq, dk, dv) = refs[:parts], refs[parts:]
        j = pl.program_id(0)
        lo, hi = first_ref[j], last_ref[j]
        here = pl.ds(pl.multiple_of(j * TILE, TILE), TILE)

        @pl.when(j == 0)
        def _():
            dq[...] = jnp.zeros(dq.shape, jnp.float32)
            for b in range(blocks):
                r, off = b * TILE // share, b * TILE % share
                base = (place_ref[0] ^ r) * share + off
                rows = pl.ds(pl.multiple_of(base, TILE), TILE)
                for h in range(heads):
                    g = g_refs[r][off : off + TILE, h * HD : (h + 1) * HD]
                    split[h, rows, :] = g
                    dots = jnp.sum(g.astype(jnp.float32) * o_ref[h, rows, :], axis=1, keepdims=True)
                    dots = jnp.transpose(jnp.broadcast_to(dots, (TILE, half)))
                    inner[h, :, rows] = dots[0:1, :]

        dk[...] = jnp.zeros(dk.shape, jnp.float32)
        dv[...] = jnp.zeros(dv.shape, jnp.float32)

        def step(i, carry):
            at = pl.ds(pl.multiple_of(i * TILE, TILE), TILE)
            same = twice(col_ref[...]) == row_ref[:, at]
            for h in range(heads):
                q, g, k = q_ref[h, at, :], split[h, at, :], k_ref[h, here, :]
                s = jnp.where(same, nt_dot(k, q), NEG)
                p = jnp.exp(s - lse_ref[h, :, at])
                dp = nt_dot(v_ref[h, here, :], g)
                ds = (p * (dp - inner[h, :, at])).astype(jnp.bfloat16)
                dv[h] = dv[h] + nn_dot(p.astype(jnp.bfloat16), g)
                dk[h] = dk[h] + nn_dot(ds, q)
                dq[h, at, :] = dq[h, at, :] + tn_dot(ds, k)
            return carry

        lax.fori_loop(lo, hi, step, 0)
        cosine, sine = c_ref[here, :], s_ref[here, :]
        for h in range(heads):
            w = dk[h]
            w = (w * cosine - swap_halves(w) * sine).astype(jnp.bfloat16)
            d_ref[here, cols + h * HD : cols + (h + 1) * HD] = w
            d_ref[here, 2 * cols + h * HD : 2 * cols + (h + 1) * HD] = dv[h].astype(jnp.bfloat16)

        @pl.when(j == blocks - 1)
        def _():
            for b in range(blocks):
                rows = slice(b * TILE, (b + 1) * TILE)
                for h in range(heads):
                    w = dq[h, rows, :] * HD**-0.5
                    w = w * c_ref[rows, :] - swap_halves(w) * s_ref[rows, :]
                    d_ref[rows, h * HD : (h + 1) * HD] = w.astype(jnp.bfloat16)

    return pl.pallas_call(
        body,
        grid_spec=pltpu.PrefetchScalarGridSpec(
            num_scalar_prefetch=3,
            grid=(blocks,),
            in_specs=[
                whole(query.shape),
                whole(key.shape),
                whole(value.shape),
                pl.BlockSpec((TILE, half), lambda i, *_: (i, 0)),
                whole(seg_row.shape),
                whole(out.shape),
                whole(lse.shape),
                whole(cos_tab.shape),
                whole(sin_tab.shape),
            ]
            + [whole(g.shape) for g in grads],
            out_specs=whole((tok_count, 3 * cols)),
            scratch_shapes=[
                pltpu.VMEM((heads, tok_count, HD), jnp.bfloat16),
                pltpu.VMEM((heads, 1, tok_count), jnp.float32),
                pltpu.VMEM((heads, tok_count, HD), jnp.float32),
                pltpu.VMEM((heads, TILE, HD), jnp.float32),
                pltpu.VMEM((heads, TILE, HD), jnp.float32),
            ],
        ),
        out_shape=jax.ShapeDtypeStruct((tok_count, 3 * cols), jnp.bfloat16),
        name="attend_grad",
    )(first, last, place, query, key, value, seg_col, seg_row, out, lse, cos_tab, sin_tab, *grads)


def swap(value, axis, step):
    count = lax.axis_size(axis)
    return lax.ppermute(value, axis, [(i, i ^ step) for i in range(count)])


def gather_far(shard):
    return [shard] + [swap(shard, "dp", step) for step in range(2, lax.axis_size("dp"), 2)]


def gather_near(pieces):
    return [v for piece in pieces for v in (piece, swap(piece, "dp", 1))]


def assemble(pieces, place, kind=None):
    count = len(pieces)
    lead, (rows, cols) = pieces[0].shape[:-2], pieces[0].shape[-2:]
    if rows % 16:
        order = place[0] ^ jnp.arange(count, dtype=jnp.int32)
        ranked = jnp.take(jnp.stack(pieces), order, axis=0)
        return jnp.moveaxis(ranked, 0, -3).reshape(*lead, count * rows, cols)

    kind = kind or pieces[0].dtype

    def body(place_ref, *refs):
        for r in range(count):
            at = pl.ds(pl.multiple_of((place_ref[0] ^ r) * rows, 16), rows)
            refs[count][(slice(None),) * len(lead) + (at, slice(None))] = refs[r][...].astype(kind)

    return pl.pallas_call(
        body,
        grid_spec=pltpu.PrefetchScalarGridSpec(
            num_scalar_prefetch=1,
            grid=(1,),
            in_specs=[whole(pieces[0].shape)] * count,
            out_specs=whole((*lead, count * rows, cols)),
        ),
        out_shape=jax.ShapeDtypeStruct((*lead, count * rows, cols), kind),
        name="assemble",
    )(place, *pieces)


def reduce_pieces(total, place):
    count = lax.axis_size("dp")
    rows, cols = total.shape[0] // count, total.shape[1]
    order = place[0] ^ jnp.array([*range(0, count, 2), *range(1, count, 2)], jnp.int32)
    ranked = jnp.take(total.reshape(count, rows, cols), order, axis=0)
    near, far = ranked[: count // 2], ranked[count // 2 :]
    near = near.astype(jnp.float32) + swap(far, "dp", 1).astype(jnp.float32)
    low = near.astype(jnp.bfloat16)
    result = near[0]
    for slot in range(1, count // 2):
        result = result + swap(low[slot], "dp", 2 * slot).astype(jnp.float32)
    return result


def layer(
    att, source, cot, gain, weight_near, weight_far, hid
):
    tok_count, width = source.shape
    head_cols = att[0].shape[1]
    parts = len(att)
    ff = parts * hid
    inner = parts * head_cols
    rows = 256

    def body(*refs):
        a_refs = refs[:parts]
        x_ref, c_ref, g_ref, wa_ref, wb_ref = refs[parts : parts + 5]
        out_ref, dmid_ref, dlow_ref, h_ref, hid_ref, dg_ref, dv_ref, gg_ref = refs[
            parts + 5 : parts + 13
        ]
        d_refs = refs[parts + 13 : 2 * parts + 13]
        gate, lift, down, proj = refs[2 * parts + 13 :]

        @pl.when(pl.program_id(0) == 0)
        def _():
            gg_ref[...] = jnp.zeros(gg_ref.shape, jnp.float32)
            for slot in range(parts):
                w_ref, s = (wa_ref, wb_ref)[slot // 2], slot % 2
                at = slice(slot * hid, (slot + 1) * hid)
                gate[:, at] = w_ref[s, :, :hid]
                lift[:, at] = w_ref[s, :, hid : 2 * hid]
                down[:, at] = w_ref[s, :, 2 * hid : 3 * hid]
                proj[:, slot * head_cols : (slot + 1) * head_cols] = w_ref[
                    s, :, 3 * hid : 3 * hid + head_cols
                ]

        gain_vec = g_ref[...]
        attended = jnp.concatenate([a_refs[r][...] for r in SLOTS], axis=1)
        mid = x_ref[...].astype(jnp.float32) + nt_dot(attended, proj[...])
        normed, factor = normalize(mid)
        h_two = (normed * gain_vec).astype(jnp.bfloat16)
        h_ref[...] = h_two
        cot_low = c_ref[...]
        first = nn_dot(h_two, gate[...])
        second = nn_dot(h_two, lift[...])
        below = 0.5 * (1.0 + lax.erf(first * math.sqrt(0.5)))
        active = first * below
        hidden = (active * second).astype(jnp.bfloat16)
        hid_ref[...] = hidden
        out_ref[...] = (mid + nt_dot(hidden, down[...])).astype(jnp.bfloat16)
        slope = below + first * (jnp.exp(-0.5 * first * first) * (1.0 / math.sqrt(2.0 * math.pi)))
        d_hidden = nn_dot(cot_low, down[...]).astype(jnp.bfloat16).astype(jnp.float32)
        d_first = (d_hidden * second * slope).astype(jnp.bfloat16)
        d_second = (d_hidden * active).astype(jnp.bfloat16)
        dg_ref[...] = d_first
        dv_ref[...] = d_second
        d_h = nt_dot(d_first, gate[...]) + nt_dot(d_second, lift[...])
        gg_ref[...] += jnp.sum(d_h * normed, axis=0, keepdims=True)
        d_mid = cot_low.astype(jnp.float32) + norm_back(d_h, normed, factor, gain_vec)
        dmid_ref[...] = d_mid
        d_low = d_mid.astype(jnp.bfloat16)
        dlow_ref[...] = d_low
        d_att = nn_dot(d_low, proj[...]).astype(jnp.bfloat16)
        for slot in range(parts):
            d_refs[SLOTS[slot]][...] = d_att[:, slot * head_cols : (slot + 1) * head_cols]

    def tile(cols):
        return pl.BlockSpec((rows, cols), lambda i: (i, 0))

    def fixed(shape):
        return pl.BlockSpec(shape, lambda *_: (0,) * len(shape), pipeline_mode=pl.Buffered(1))

    def shape(cols, kind=jnp.bfloat16):
        return jax.ShapeDtypeStruct((tok_count, cols), kind)

    return pl.pallas_call(
        body,
        grid=(tok_count // rows,),
        in_specs=[tile(head_cols)] * parts
        + [tile(width), tile(width), whole((1, width))]
        + [fixed(weight_near.shape), fixed(weight_far.shape)],
        out_specs=[tile(width)] * 4
        + [tile(ff)] * 3
        + [whole((1, width))]
        + [tile(head_cols)] * parts,
        out_shape=[
            shape(width),
            shape(width, jnp.float32),
            shape(width),
            shape(width),
            shape(ff),
            shape(ff),
            shape(ff),
            jax.ShapeDtypeStruct((1, width), jnp.float32),
        ]
        + [shape(head_cols)] * parts,
        scratch_shapes=[
            pltpu.VMEM((width, ff), jnp.bfloat16),
            pltpu.VMEM((width, ff), jnp.bfloat16),
            pltpu.VMEM((width, ff), jnp.bfloat16),
            pltpu.VMEM((width, inner), jnp.bfloat16),
        ],
        name="layer",
    )(*att, source, cot, gain[None, :], weight_near, weight_far)


SLOTS = (0, 2, 1, 3)


def weight_grads(side, h_two, d_first, d_second, cot, hidden, d_low, att, gain_grad, wide):
    tok_count, width = h_two.shape
    hid = hidden.shape[1] // len(SLOTS)
    head_cols = att[0].shape[1]
    both = tuple(att[r] for r in SLOTS[2 * side : 2 * side + 2])
    here = slice(2 * side * hid, (2 * side + 2) * hid)

    def body(h_ref, f_ref, s_ref, c_ref, u_ref, l_ref, a_ref, b_ref, g_ref, out_ref):
        for ref, turned, at in ((f_ref, h_ref, 0), (s_ref, h_ref, hid), (u_ref, c_ref, 2 * hid)):
            full = tn_dot(turned[...], ref[:, here]).astype(jnp.bfloat16)
            out_ref[0, :, at : at + hid] = full[:, :hid]
            out_ref[1, :, at : at + hid] = full[:, hid:]
        gain_col = jnp.transpose(jnp.broadcast_to(g_ref[...], (128, width))).astype(jnp.bfloat16)
        for s, ref in ((0, a_ref), (1, b_ref)):
            at = 3 * hid
            out_ref[s, :, at : at + head_cols] = tn_dot(l_ref[...], ref[...]).astype(jnp.bfloat16)
            out_ref[s, :, at + head_cols :] = gain_col[:, : wide - at - head_cols]

    return pl.pallas_call(
        body,
        out_shape=jax.ShapeDtypeStruct((2, width, wide), jnp.bfloat16),
        name="weight_grads",
    )(h_two, d_first, d_second, cot, hidden, d_low, *both, gain_grad)


def back_to_width(d_qkv, weight, place, slots, share):
    width, cols = weight.shape
    first, stride = slots[0], slots[1] - slots[0]

    def body(place_ref, d_ref, w_ref, out_ref):
        out_ref[0] = nt_dot(d_ref[...], w_ref[...]).astype(jnp.bfloat16)

    return pl.pallas_call(
        body,
        grid_spec=pltpu.PrefetchScalarGridSpec(
            num_scalar_prefetch=1,
            grid=(len(slots),),
            in_specs=[
                pl.BlockSpec((share, cols), lambda i, at: (at[0] ^ (first + stride * i), 0)),
                whole(weight.shape),
            ],
            out_specs=pl.BlockSpec((1, share, width), lambda i, at: (i, 0, 0)),
        ),
        out_shape=jax.ShapeDtypeStruct((len(slots), share, width), jnp.bfloat16),
        name="back_to_width",
    )(place, d_qkv, weight)


def share_rows(mine, place, kind=None):
    other = swap(mine, "tensor", 2)
    far = swap(jnp.stack([mine, other]), "tensor", 1)
    return assemble([mine, far[0], other, far[1]], place, kind)


def shards(
    tokens, lengths, attn_gain, qkv_weight, out_weight, mlp_gain, up_weight, down_weight, cotangent
):
    tok_count, width = tokens.shape
    parts = lax.axis_size("tensor")
    share = tok_count // parts
    rank = lax.axis_index("tensor").astype(jnp.int32)
    place = rank[None]
    dp_place = lax.axis_index("dp").astype(jnp.int32)[None]
    rows = qkv_weight.shape[0]
    head_cols = qkv_weight.shape[2]
    heads_dev = head_cols // HD
    hid = up_weight.shape[2]
    used = 3 * hid + head_cols
    wide = used // 128 * 128 + 128

    qkv_far = gather_far(qkv_weight.reshape(rows, 3 * head_cols))
    qkv_flat = assemble(gather_near(qkv_far), dp_place)
    packed = jnp.concatenate(
        [
            up_weight.reshape(rows, 2 * hid),
            down_weight.T,
            out_weight.T,
            jnp.zeros((rows, wide - used), jnp.bfloat16),
        ],
        axis=1,
    )
    paired = jnp.stack([packed, swap(packed, "tensor", 2)])
    paired, _ = lax.optimization_barrier((paired, qkv_far))
    weight_near = assemble(gather_near(gather_far(paired)), dp_place)
    weight_far = swap(weight_near, "tensor", 1)

    segment, position = row_layout(lengths[0], tok_count)
    cosine, sine_table = rotary_tables(position, HD)
    h_one = (normalize(tokens.astype(jnp.float32))[0] * attn_gain).astype(jnp.bfloat16)
    seg_col = jnp.broadcast_to(segment[:, None], (tok_count, TILE // 2))
    seg_row = segment[None, :]
    first, last = tile_ranges(lengths[0], tok_count)
    query, key, value = project_heads(h_one, qkv_flat, cosine, sine_table, heads_dev)
    *sent, attended_wide, log_total = attend(
        first, last, place, query, key, value, seg_col, seg_row, parts
    )
    att = [sent[0]] + [swap(sent[r], "tensor", r) for r in range(1, parts)]
    my_tokens = lax.dynamic_slice_in_dim(tokens, rank * share, share, 0)
    my_cot = lax.dynamic_slice_in_dim(cotangent, rank * share, share, 0)
    out, d_mid, d_low, h_two, hidden, d_first, d_second, gain_two, *d_sent = layer(
        att, my_tokens, my_cot, mlp_gain, weight_near, weight_far, hid
    )
    d_att = [d_sent[0]] + [swap(d_sent[r], "tensor", r) for r in range(1, parts)]
    output = share_rows(out, place)

    grads_in = (h_two, d_first, d_second, my_cot, hidden, d_low, att, gain_two, wide)
    grads_far = weight_grads(1, *grads_in)
    grads_near = weight_grads(0, *grads_in)
    chip = grads_near.astype(jnp.float32) + swap(grads_far, "tensor", 1).astype(jnp.float32)
    chip_sent, d_att = lax.optimization_barrier((chip[1].astype(jnp.bfloat16), d_att))
    column = chip[0] + swap(chip_sent, "tensor", 2).astype(jnp.float32)
    reduced = reduce_pieces(column.astype(jnp.bfloat16), dp_place)
    up_grad = reduced[:, : 2 * hid].reshape(rows, 2, hid)
    down_grad = reduced[:, 2 * hid : 3 * hid].T
    out_grad = reduced[:, 3 * hid : used].T
    mlp_gain_grad = reduced[:, used]

    d_qkv = attend_grad(
        first,
        last,
        place,
        query,
        key,
        value,
        seg_col,
        seg_row,
        d_att,
        attended_wide,
        log_total,
        cosine,
        sine_table,
    )
    d_far = back_to_width(d_qkv, qkv_flat, place, (1, 3), share)
    d_near = back_to_width(d_qkv, qkv_flat, place, (0, 2), share)
    d_chip = d_near.astype(jnp.float32) + swap(d_far, "tensor", 1).astype(jnp.float32)
    d_h_one = d_chip[0] + swap(d_chip[1].astype(jnp.bfloat16), "tensor", 2).astype(jnp.float32)
    normed_one, factor_one = normalize(my_tokens.astype(jnp.float32))
    tokens_grad = d_mid + norm_back(d_h_one, normed_one, factor_one, attn_gain)
    tokens_grad = share_rows(tokens_grad.astype(jnp.bfloat16), place, jnp.float32)
    gain_one = jnp.sum(d_h_one * normed_one, axis=0)[None, :]
    gain_one = gain_one + sum(swap(gain_one, "tensor", r) for r in range(1, parts))
    gain_one = gain_one + sum(swap(gain_one, "dp", r) for r in range(1, lax.axis_size("dp")))
    attn_gain_grad = lax.dynamic_slice_in_dim(gain_one[0], dp_place[0] * rows, rows, 0)
    qkv_total = jnp.einsum("td,tf->df", h_one, d_qkv, preferred_element_type=jnp.float32)
    qkv_grad = reduce_pieces(qkv_total.astype(jnp.bfloat16), dp_place).reshape(rows, 3, head_cols)
    return (
        output,
        tokens_grad,
        attn_gain_grad,
        qkv_grad,
        out_grad,
        mlp_gain_grad,
        up_grad,
        down_grad,
    )


def solution(mesh):
    in_specs = (
        P("dp", None),
        P("dp", None),
        P(),
        P("dp", None, "tensor"),
        P("tensor", "dp"),
        P(),
        P("dp", None, "tensor"),
        P("tensor", "dp"),
        P("dp", None),
    )
    out_specs = (
        P("dp", None),
        P("dp", None),
        P("dp"),
        P("dp", None, "tensor"),
        P("tensor", "dp"),
        P("dp"),
        P("dp", None, "tensor"),
        P("tensor", "dp"),
    )
    return jax.shard_map(shards, mesh=mesh, in_specs=in_specs, out_specs=out_specs, check_vma=False)
```

```python
import math

import jax
import jax.numpy as jnp
from jax import lax
from jax.experimental import pallas as pl
from jax.experimental.pallas import tpu as pltpu
from jax.sharding import PartitionSpec as P

HD = 64

eps_norm = 1e-05
theta_base = 160000.0


def row_layout(row_lengths, tok_count):
    doc_ends = jnp.cumsum(row_lengths, dtype=jnp.int32)
    tok_place = jnp.arange(tok_count, dtype=jnp.int32)
    passed = tok_place[:, None] >= doc_ends[None, :]
    segment = jnp.sum(passed.astype(jnp.int32), axis=1, dtype=jnp.int32)
    doc_start = jnp.sum(jnp.where(passed, row_lengths[None, :], 0), axis=1, dtype=jnp.int32)
    return (segment, tok_place - doc_start)


def tile_ranges(row_lengths, tok_count):
    ends = jnp.cumsum(row_lengths, dtype=jnp.int32)
    starts = ends - row_lengths
    begin = jnp.arange(tok_count // TILE, dtype=jnp.int32)[:, None] * TILE
    touched = (ends[None, :] > begin) & (starts[None, :] < begin + TILE)
    low = jnp.min(jnp.where(touched, starts[None, :], tok_count), axis=1)
    high = jnp.max(jnp.where(touched, ends[None, :], 0), axis=1)
    return (low // TILE, (high + TILE - 1) // TILE)


def rotary_tables(position, head_width):
    half_width = head_width // 2
    freq_index = jnp.arange(half_width, dtype=jnp.float32)
    inv_freq = jnp.exp(freq_index * (-2.0 * math.log(theta_base) / head_width))
    angles = position.astype(jnp.float32)[:, None] * inv_freq[None, :]
    cosine, sine = jnp.cos(angles), jnp.sin(angles)
    return (jnp.concatenate([cosine, cosine], axis=1), jnp.concatenate([-sine, sine], axis=1))


def normalize(vector):
    row_mean = jnp.mean(vector, axis=-1, keepdims=True)
    centred = vector - row_mean
    spread = jnp.mean(centred * centred, axis=-1, keepdims=True)
    factor = lax.rsqrt(spread + eps_norm)
    return (centred * factor, factor)


def norm_back(grad_norm_out, normed, factor, gain_vec):
    grad_normed = grad_norm_out * gain_vec
    first_mean = jnp.mean(grad_normed, axis=-1, keepdims=True)
    second_mean = jnp.mean(grad_normed * normed, axis=-1, keepdims=True)
    return factor * (grad_normed - first_mean - normed * second_mean)


TILE = 256
NEG = -1e30


def nt_dot(a, b):
    return lax.dot_general(a, b, (((1,), (1,)), ((), ())), preferred_element_type=jnp.float32)


def nn_dot(a, b):
    return lax.dot_general(a, b, (((1,), (0,)), ((), ())), preferred_element_type=jnp.float32)


def tn_dot(a, b):
    return lax.dot_general(a, b, (((0,), (0,)), ((), ())), preferred_element_type=jnp.float32)


def swap_halves(u):
    half = u.shape[-1] // 2
    return jnp.concatenate([u[:, half:], u[:, :half]], axis=1)


def twice(a):
    return jnp.concatenate([a, a], axis=1)


def lane_fold(op, a):
    return op(a[:, : TILE // 2], a[:, TILE // 2 :])


def whole(shape):
    return pl.BlockSpec(shape, lambda *_: (0,) * len(shape))


def project_heads(h_one, weight, cos_tab, sin_tab, heads):
    tok_count, width = h_one.shape
    cols = heads * HD
    rows = 2 * TILE

    def body(h_ref, w_ref, c_ref, s_ref, q_ref, k_ref, v_ref):
        full = nn_dot(h_ref[...], w_ref[...])
        cosine, sine = c_ref[...], s_ref[...]
        for h in range(heads):
            u = full[:, h * HD : (h + 1) * HD]
            turned = (u * cosine + swap_halves(u) * sine).astype(jnp.bfloat16)
            q_ref[h] = (turned.astype(jnp.float32) * HD**-0.5).astype(jnp.bfloat16)
            u = full[:, cols + h * HD : cols + (h + 1) * HD]
            k_ref[h] = (u * cosine + swap_halves(u) * sine).astype(jnp.bfloat16)
            v_ref[h] = full[:, 2 * cols + h * HD : 2 * cols + (h + 1) * HD].astype(jnp.bfloat16)

    out = jax.ShapeDtypeStruct((heads, tok_count, HD), jnp.bfloat16)
    return pl.pallas_call(
        body,
        grid=(tok_count // rows,),
        in_specs=[
            pl.BlockSpec((rows, width), lambda i: (i, 0)),
            whole(weight.shape),
            pl.BlockSpec((rows, HD), lambda i: (i, 0)),
            pl.BlockSpec((rows, HD), lambda i: (i, 0)),
        ],
        out_specs=[pl.BlockSpec((heads, rows, HD), lambda i: (0, i, 0))] * 3,
        out_shape=[out] * 3,
        name="project_heads",
    )(h_one, weight, cos_tab, sin_tab)


def attend(first, last, place, query, key, value, seg_col, seg_row, parts):
    heads, tok_count, _ = query.shape
    blocks = tok_count // TILE
    share = blocks // parts
    half = TILE // 2

    def body(
        first_ref, last_ref, place_ref, q_ref, k_ref, v_ref, col_ref, row_ref, *refs
    ):
        low_refs, (out_ref, lse_ref, scores, peak, total, accum, low) = refs[:parts], refs[parts:]
        i = pl.program_id(0)
        lo, hi = first_ref[i], last_ref[i]
        peak[...] = jnp.full(peak.shape, NEG, jnp.float32)
        total[...] = jnp.zeros(total.shape, jnp.float32)
        accum[...] = jnp.zeros(accum.shape, jnp.float32)

        def score(j, carry):
            at = pl.multiple_of(j * TILE, TILE)
            same = twice(col_ref[...]) == row_ref[:, pl.ds(at, TILE)]
            for h in range(heads):
                s = jnp.where(same, nt_dot(q_ref[h], k_ref[h, pl.ds(at, TILE), :]), NEG)
                scores[h, j] = s
                peak[h] = jnp.maximum(peak[h], lane_fold(jnp.maximum, s))
            return carry

        lax.fori_loop(lo, hi, score, 0)
        for h in range(heads):
            peak[h] = jnp.broadcast_to(jnp.max(peak[h], axis=1, keepdims=True), (TILE, half))

        def spread(j, carry):
            at = pl.multiple_of(j * TILE, TILE)
            for h in range(heads):
                p = jnp.exp(scores[h, j] - twice(peak[h]))
                total[h] = total[h] + lane_fold(jnp.add, p)
                accum[h] = accum[h] + nn_dot(p.astype(jnp.bfloat16), v_ref[h, pl.ds(at, TILE), :])
            return carry

        lax.fori_loop(lo, hi, spread, 0)
        for h in range(heads):
            norm = jnp.sum(total[h], axis=1, keepdims=True)
            out = accum[h] / norm
            out_ref[h] = out
            low[:, h * HD : (h + 1) * HD] = out.astype(jnp.bfloat16)
            logs = peak[h] + jnp.log(jnp.broadcast_to(norm, (TILE, half)))
            lse_ref[h] = jnp.transpose(logs)[0:1, :]
        rows = pl.ds(pl.multiple_of((i % share) * TILE, TILE), TILE)
        for r in range(parts):

            @pl.when((i // share) ^ place_ref[0] == r)
            def _():
                low_refs[r][rows, :] = low[...]

    tile = pl.BlockSpec((heads, TILE, HD), lambda i, *_: (0, i, 0))
    return pl.pallas_call(
        body,
        grid_spec=pltpu.PrefetchScalarGridSpec(
            num_scalar_prefetch=3,
            grid=(blocks,),
            in_specs=[
                tile,
                whole(key.shape),
                whole(value.shape),
                pl.BlockSpec((TILE, half), lambda i, *_: (i, 0)),
                whole(seg_row.shape),
            ],
            out_specs=[whole((share * TILE, heads * HD))] * parts
            + [
                tile,
                pl.BlockSpec((heads, 1, TILE), lambda i, *_: (0, 0, i)),
            ],
            scratch_shapes=[
                pltpu.VMEM((heads, blocks, TILE, TILE), jnp.float32),
                pltpu.VMEM((heads, TILE, half), jnp.float32),
                pltpu.VMEM((heads, TILE, half), jnp.float32),
                pltpu.VMEM((heads, TILE, HD), jnp.float32),
                pltpu.VMEM((TILE, heads * HD), jnp.bfloat16),
            ],
        ),
        out_shape=[jax.ShapeDtypeStruct((share * TILE, heads * HD), jnp.bfloat16)] * parts
        + [
            jax.ShapeDtypeStruct((heads, tok_count, HD), jnp.float32),
            jax.ShapeDtypeStruct((heads, 1, tok_count), jnp.float32),
        ],
        name="attend",
    )(first, last, place, query, key, value, seg_col, seg_row)


def attend_grad(
    first, last, place, query, key, value, seg_col, seg_row, grads, out, lse, cos_tab, sin_tab
):
    heads, tok_count, _ = query.shape
    blocks = tok_count // TILE
    half = TILE // 2
    cols = heads * HD
    parts = len(grads)
    share = tok_count // parts

    def body(
        first_ref, last_ref, place_ref, q_ref, k_ref, v_ref, col_ref, row_ref, o_ref, lse_ref,
        c_ref, s_ref, *refs
    ):
        g_refs, (d_ref, split, inner, dq, dk, dv) = refs[:parts], refs[parts:]
        j = pl.program_id(0)
        lo, hi = first_ref[j], last_ref[j]
        here = pl.ds(pl.multiple_of(j * TILE, TILE), TILE)

        @pl.when(j == 0)
        def _():
            dq[...] = jnp.zeros(dq.shape, jnp.float32)
            for b in range(blocks):
                r, off = b * TILE // share, b * TILE % share
                base = (place_ref[0] ^ r) * share + off
                rows = pl.ds(pl.multiple_of(base, TILE), TILE)
                for h in range(heads):
                    g = g_refs[r][off : off + TILE, h * HD : (h + 1) * HD]
                    split[h, rows, :] = g
                    dots = jnp.sum(g.astype(jnp.float32) * o_ref[h, rows, :], axis=1, keepdims=True)
                    dots = jnp.transpose(jnp.broadcast_to(dots, (TILE, half)))
                    inner[h, :, rows] = dots[0:1, :]

        dk[...] = jnp.zeros(dk.shape, jnp.float32)
        dv[...] = jnp.zeros(dv.shape, jnp.float32)

        def step(i, carry):
            at = pl.ds(pl.multiple_of(i * TILE, TILE), TILE)
            same = twice(col_ref[...]) == row_ref[:, at]
            for h in range(heads):
                q, g, k = q_ref[h, at, :], split[h, at, :], k_ref[h, here, :]
                s = jnp.where(same, nt_dot(k, q), NEG)
                p = jnp.exp(s - lse_ref[h, :, at])
                dp = nt_dot(v_ref[h, here, :], g)
                ds = (p * (dp - inner[h, :, at])).astype(jnp.bfloat16)
                dv[h] = dv[h] + nn_dot(p.astype(jnp.bfloat16), g)
                dk[h] = dk[h] + nn_dot(ds, q)
                dq[h, at, :] = dq[h, at, :] + tn_dot(ds, k)
            return carry

        lax.fori_loop(lo, hi, step, 0)
        cosine, sine = c_ref[here, :], s_ref[here, :]
        for h in range(heads):
            w = dk[h]
            w = (w * cosine - swap_halves(w) * sine).astype(jnp.bfloat16)
            d_ref[here, cols + h * HD : cols + (h + 1) * HD] = w
            d_ref[here, 2 * cols + h * HD : 2 * cols + (h + 1) * HD] = dv[h].astype(jnp.bfloat16)

        @pl.when(j == blocks - 1)
        def _():
            for b in range(blocks):
                rows = slice(b * TILE, (b + 1) * TILE)
                for h in range(heads):
                    w = dq[h, rows, :] * HD**-0.5
                    w = w * c_ref[rows, :] - swap_halves(w) * s_ref[rows, :]
                    d_ref[rows, h * HD : (h + 1) * HD] = w.astype(jnp.bfloat16)

    return pl.pallas_call(
        body,
        grid_spec=pltpu.PrefetchScalarGridSpec(
            num_scalar_prefetch=3,
            grid=(blocks,),
            in_specs=[
                whole(query.shape),
                whole(key.shape),
                whole(value.shape),
                pl.BlockSpec((TILE, half), lambda i, *_: (i, 0)),
                whole(seg_row.shape),
                whole(out.shape),
                whole(lse.shape),
                whole(cos_tab.shape),
                whole(sin_tab.shape),
            ]
            + [whole(g.shape) for g in grads],
            out_specs=whole((tok_count, 3 * cols)),
            scratch_shapes=[
                pltpu.VMEM((heads, tok_count, HD), jnp.bfloat16),
                pltpu.VMEM((heads, 1, tok_count), jnp.float32),
                pltpu.VMEM((heads, tok_count, HD), jnp.float32),
                pltpu.VMEM((heads, TILE, HD), jnp.float32),
                pltpu.VMEM((heads, TILE, HD), jnp.float32),
            ],
        ),
        out_shape=jax.ShapeDtypeStruct((tok_count, 3 * cols), jnp.bfloat16),
        name="attend_grad",
    )(first, last, place, query, key, value, seg_col, seg_row, out, lse, cos_tab, sin_tab, *grads)


def swap(value, axis, step):
    count = lax.axis_size(axis)
    return lax.ppermute(value, axis, [(i, i ^ step) for i in range(count)])


def gather_far(shard):
    return [shard] + [swap(shard, "dp", step) for step in range(2, lax.axis_size("dp"), 2)]


def gather_near(pieces):
    return [v for piece in pieces for v in (piece, swap(piece, "dp", 1))]


def assemble(pieces, place, kind=None):
    count = len(pieces)
    lead, (rows, cols) = pieces[0].shape[:-2], pieces[0].shape[-2:]
    if rows % 16:
        order = place[0] ^ jnp.arange(count, dtype=jnp.int32)
        ranked = jnp.take(jnp.stack(pieces), order, axis=0)
        return jnp.moveaxis(ranked, 0, -3).reshape(*lead, count * rows, cols)

    kind = kind or pieces[0].dtype

    def body(place_ref, *refs):
        for r in range(count):
            at = pl.ds(pl.multiple_of((place_ref[0] ^ r) * rows, 16), rows)
            refs[count][(slice(None),) * len(lead) + (at, slice(None))] = refs[r][...].astype(kind)

    return pl.pallas_call(
        body,
        grid_spec=pltpu.PrefetchScalarGridSpec(
            num_scalar_prefetch=1,
            grid=(1,),
            in_specs=[whole(pieces[0].shape)] * count,
            out_specs=whole((*lead, count * rows, cols)),
        ),
        out_shape=jax.ShapeDtypeStruct((*lead, count * rows, cols), kind),
        name="assemble",
    )(place, *pieces)


def reduce_near(total, place):
    count = lax.axis_size("dp")
    rows, cols = total.shape[0] // count, total.shape[1]
    order = place[0] ^ jnp.array([*range(0, count, 2), *range(1, count, 2)], jnp.int32)
    ranked = jnp.take(total.reshape(count, rows, cols), order, axis=0)
    return ranked[: count // 2], swap(ranked[count // 2 :], "dp", 1)


def reduce_far(near, come):
    near = near.astype(jnp.float32) + come.astype(jnp.float32)
    low = near.astype(jnp.bfloat16)
    result = near[0]
    for slot in range(1, near.shape[0]):
        result = result + swap(low[slot], "dp", 2 * slot).astype(jnp.float32)
    return result


def layer(
    att, source, cot, gain, weight_near, weight_far, hid
):
    tok_count, width = source.shape
    head_cols = att[0].shape[1]
    parts = len(att)
    ff = parts * hid
    inner = parts * head_cols
    rows = 256

    def body(*refs):
        a_refs = refs[:parts]
        x_ref, c_ref, g_ref, wa_ref, wb_ref = refs[parts : parts + 5]
        out_ref, dmid_ref, dlow_ref, h_ref, hid_ref, dg_ref, dv_ref, gg_ref = refs[
            parts + 5 : parts + 13
        ]
        d_refs = refs[parts + 13 : 2 * parts + 13]
        gate, lift, down, proj = refs[2 * parts + 13 :]

        @pl.when(pl.program_id(0) == 0)
        def _():
            gg_ref[...] = jnp.zeros(gg_ref.shape, jnp.float32)
            for slot in range(parts):
                w_ref, s = (wa_ref, wb_ref)[slot // 2], slot % 2
                at = slice(slot * hid, (slot + 1) * hid)
                gate[:, at] = w_ref[s, :, :hid]
                lift[:, at] = w_ref[s, :, hid : 2 * hid]
                down[:, at] = w_ref[s, :, 2 * hid : 3 * hid]
                proj[:, slot * head_cols : (slot + 1) * head_cols] = w_ref[
                    s, :, 3 * hid : 3 * hid + head_cols
                ]

        gain_vec = g_ref[...]
        attended = jnp.concatenate([a_refs[r][...] for r in SLOTS], axis=1)
        mid = x_ref[...].astype(jnp.float32) + nt_dot(attended, proj[...])
        normed, factor = normalize(mid)
        h_two = (normed * gain_vec).astype(jnp.bfloat16)
        h_ref[...] = h_two
        cot_low = c_ref[...]
        first = nn_dot(h_two, gate[...])
        second = nn_dot(h_two, lift[...])
        below = 0.5 * (1.0 + lax.erf(first * math.sqrt(0.5)))
        active = first * below
        hidden = (active * second).astype(jnp.bfloat16)
        hid_ref[...] = hidden
        out_ref[...] = (mid + nt_dot(hidden, down[...])).astype(jnp.bfloat16)
        slope = below + first * (jnp.exp(-0.5 * first * first) * (1.0 / math.sqrt(2.0 * math.pi)))
        d_hidden = nn_dot(cot_low, down[...]).astype(jnp.bfloat16).astype(jnp.float32)
        d_first = (d_hidden * second * slope).astype(jnp.bfloat16)
        d_second = (d_hidden * active).astype(jnp.bfloat16)
        dg_ref[...] = d_first
        dv_ref[...] = d_second
        d_h = nt_dot(d_first, gate[...]) + nt_dot(d_second, lift[...])
        gg_ref[...] += jnp.sum(d_h * normed, axis=0, keepdims=True)
        d_mid = cot_low.astype(jnp.float32) + norm_back(d_h, normed, factor, gain_vec)
        dmid_ref[...] = d_mid
        d_low = d_mid.astype(jnp.bfloat16)
        dlow_ref[...] = d_low
        d_att = nn_dot(d_low, proj[...]).astype(jnp.bfloat16)
        for slot in range(parts):
            d_refs[SLOTS[slot]][...] = d_att[:, slot * head_cols : (slot + 1) * head_cols]

    def tile(cols):
        return pl.BlockSpec((rows, cols), lambda i: (i, 0))

    def fixed(shape):
        return pl.BlockSpec(shape, lambda *_: (0,) * len(shape), pipeline_mode=pl.Buffered(1))

    def shape(cols, kind=jnp.bfloat16):
        return jax.ShapeDtypeStruct((tok_count, cols), kind)

    return pl.pallas_call(
        body,
        grid=(tok_count // rows,),
        in_specs=[tile(head_cols)] * parts
        + [tile(width), tile(width), whole((1, width))]
        + [fixed(weight_near.shape), fixed(weight_far.shape)],
        out_specs=[tile(width)] * 4
        + [tile(ff)] * 3
        + [whole((1, width))]
        + [tile(head_cols)] * parts,
        out_shape=[
            shape(width),
            shape(width, jnp.float32),
            shape(width),
            shape(width),
            shape(ff),
            shape(ff),
            shape(ff),
            jax.ShapeDtypeStruct((1, width), jnp.float32),
        ]
        + [shape(head_cols)] * parts,
        scratch_shapes=[
            pltpu.VMEM((width, ff), jnp.bfloat16),
            pltpu.VMEM((width, ff), jnp.bfloat16),
            pltpu.VMEM((width, ff), jnp.bfloat16),
            pltpu.VMEM((width, inner), jnp.bfloat16),
        ],
        name="layer",
    )(*att, source, cot, gain[None, :], weight_near, weight_far)


SLOTS = (0, 2, 1, 3)


def weight_grads(side, h_two, d_first, d_second, cot, hidden, d_low, att, gain_grad, wide):
    _, width = h_two.shape
    hid = hidden.shape[1] // len(SLOTS)
    head_cols = att[0].shape[1]
    both = tuple(att[r] for r in SLOTS[2 * side : 2 * side + 2])
    here = slice(2 * side * hid, (2 * side + 2) * hid)

    def body(h_ref, f_ref, s_ref, c_ref, u_ref, l_ref, a_ref, b_ref, g_ref, out_ref):
        for ref, turned, at in ((f_ref, h_ref, 0), (s_ref, h_ref, hid), (u_ref, c_ref, 2 * hid)):
            full = tn_dot(turned[...], ref[:, here]).astype(jnp.bfloat16)
            out_ref[0, :, at : at + hid] = full[:, :hid]
            out_ref[1, :, at : at + hid] = full[:, hid:]
        gain_col = jnp.transpose(jnp.broadcast_to(g_ref[...], (128, width))).astype(jnp.bfloat16)
        for s, ref in ((0, a_ref), (1, b_ref)):
            at = 3 * hid
            out_ref[s, :, at : at + head_cols] = tn_dot(l_ref[...], ref[...]).astype(jnp.bfloat16)
            out_ref[s, :, at + head_cols :] = gain_col[:, : wide - at - head_cols]

    return pl.pallas_call(
        body,
        out_shape=jax.ShapeDtypeStruct((2, width, wide), jnp.bfloat16),
        name="weight_grads",
    )(h_two, d_first, d_second, cot, hidden, d_low, *both, gain_grad)


def back_to_width(d_qkv, weight, place, slots, share):
    width, cols = weight.shape
    first, stride = slots[0], slots[1] - slots[0]

    def body(place_ref, d_ref, w_ref, out_ref):
        out_ref[0] = nt_dot(d_ref[...], w_ref[...]).astype(jnp.bfloat16)

    return pl.pallas_call(
        body,
        grid_spec=pltpu.PrefetchScalarGridSpec(
            num_scalar_prefetch=1,
            grid=(len(slots),),
            in_specs=[
                pl.BlockSpec((share, cols), lambda i, at: (at[0] ^ (first + stride * i), 0)),
                whole(weight.shape),
            ],
            out_specs=pl.BlockSpec((1, share, width), lambda i, at: (i, 0, 0)),
        ),
        out_shape=jax.ShapeDtypeStruct((len(slots), share, width), jnp.bfloat16),
        name="back_to_width",
    )(place, d_qkv, weight)


def share_rows(mine, place, kind=None):
    other = swap(mine, "tensor", 2)
    far = swap(jnp.stack([mine, other]), "tensor", 1)
    return assemble([mine, far[0], other, far[1]], place, kind)


def layer_shards(
    tokens, lengths, attn_gain, qkv_weight, out_weight, mlp_gain, up_weight, down_weight, cotangent
):
    tok_count, _ = tokens.shape
    parts = lax.axis_size("tensor")
    share = tok_count // parts
    rank = lax.axis_index("tensor").astype(jnp.int32)
    place = rank[None]
    dp_place = lax.axis_index("dp").astype(jnp.int32)[None]
    rows = qkv_weight.shape[0]
    head_cols = qkv_weight.shape[2]
    heads_dev = head_cols // HD
    hid = up_weight.shape[2]
    used = 3 * hid + head_cols
    wide = used // 128 * 128 + 128

    qkv_own = qkv_weight.reshape(rows, 3 * head_cols)
    qkv_own, up_weight, down_weight, out_weight = lax.optimization_barrier(
        (qkv_own, up_weight, down_weight, out_weight)
    )
    qkv_far = gather_far(qkv_own)
    qkv_flat = assemble(gather_near(qkv_far), dp_place)
    packed = jnp.concatenate(
        [
            up_weight.reshape(rows, 2 * hid),
            down_weight.T,
            out_weight.T,
            jnp.zeros((rows, wide - used), jnp.bfloat16),
        ],
        axis=1,
    )
    paired = jnp.stack([packed, swap(packed, "tensor", 2)])
    paired, _ = lax.optimization_barrier((paired, qkv_far))
    paired_far = gather_far(paired)

    segment, position = row_layout(lengths[0], tok_count)
    cosine, sine_table = rotary_tables(position, HD)
    h_one = (normalize(tokens.astype(jnp.float32))[0] * attn_gain).astype(jnp.bfloat16)
    seg_col = jnp.broadcast_to(segment[:, None], (tok_count, TILE // 2))
    seg_row = segment[None, :]
    first, last = tile_ranges(lengths[0], tok_count)
    query, key, value = project_heads(h_one, qkv_flat, cosine, sine_table, heads_dev)
    paired_far, query = lax.optimization_barrier((paired_far, query))
    pieces = gather_near(paired_far)
    *sent, attended_wide, log_total = attend(
        first, last, place, query, key, value, seg_col, seg_row, parts
    )
    sent, pieces = lax.optimization_barrier((sent, pieces))
    weight_near = assemble(pieces, dp_place)
    weight_far = swap(weight_near, "tensor", 1)
    att = [sent[0]] + [swap(sent[r], "tensor", r) for r in range(1, parts)]
    my_tokens = lax.dynamic_slice_in_dim(tokens, rank * share, share, 0)
    my_cot = lax.dynamic_slice_in_dim(cotangent, rank * share, share, 0)
    out, d_mid, d_low, h_two, hidden, d_first, d_second, gain_two, *d_sent = layer(
        att, my_tokens, my_cot, mlp_gain, weight_near, weight_far, hid
    )
    d_att = [d_sent[0]] + [swap(d_sent[r], "tensor", r) for r in range(1, parts)]
    output = share_rows(out, place)

    grads_in = (h_two, d_first, d_second, my_cot, hidden, d_low, att, gain_two, wide)
    grads_far = weight_grads(1, *grads_in)
    grads_near = weight_grads(0, *grads_in)
    chip = grads_near.astype(jnp.float32) + swap(grads_far, "tensor", 1).astype(jnp.float32)
    chip_sent, d_att = lax.optimization_barrier((chip[1].astype(jnp.bfloat16), d_att))
    column_come = swap(chip_sent, "tensor", 2)

    d_qkv = attend_grad(
        first,
        last,
        place,
        query,
        key,
        value,
        seg_col,
        seg_row,
        d_att,
        attended_wide,
        log_total,
        cosine,
        sine_table,
    )
    d_far = back_to_width(d_qkv, qkv_flat, place, (1, 3), share)
    d_near = back_to_width(d_qkv, qkv_flat, place, (0, 2), share)
    d_chip = d_near.astype(jnp.float32) + swap(d_far, "tensor", 1).astype(jnp.float32)
    d_sent, d_qkv, column_come = lax.optimization_barrier(
        (d_chip[1].astype(jnp.bfloat16), d_qkv, column_come)
    )
    d_come = swap(d_sent, "tensor", 2)
    column = (chip[0] + column_come.astype(jnp.float32)).astype(jnp.bfloat16)
    column_near, column_come = reduce_near(column, dp_place)
    qkv_total = jnp.einsum("td,tf->df", h_one, d_qkv, preferred_element_type=jnp.float32)
    qkv_near, qkv_come = reduce_near(qkv_total.astype(jnp.bfloat16), dp_place)
    normed_one, factor_one = normalize(my_tokens.astype(jnp.float32))
    d_h_one = d_chip[0] + d_come.astype(jnp.float32)
    tokens_grad = d_mid + norm_back(d_h_one, normed_one, factor_one, attn_gain)
    tokens_grad, column_come, qkv_come = lax.optimization_barrier(
        (tokens_grad.astype(jnp.bfloat16), column_come, qkv_come)
    )
    tokens_grad = share_rows(tokens_grad, place, jnp.float32)
    reduced = reduce_far(column_near, column_come)
    up_grad = reduced[:, : 2 * hid].reshape(rows, 2, hid)
    down_grad = reduced[:, 2 * hid : 3 * hid].T
    out_grad = reduced[:, 3 * hid : used].T
    mlp_gain_grad = reduced[:, used]
    qkv_grad = reduce_far(qkv_near, qkv_come)
    gain_one = jnp.sum(qkv_grad * qkv_own.astype(jnp.float32), axis=1)
    gain_one = gain_one + sum(swap(gain_one, "tensor", r) for r in range(1, parts))
    attn_gain_grad = gain_one / lax.dynamic_slice_in_dim(attn_gain, dp_place[0] * rows, rows, 0)
    qkv_grad = qkv_grad.reshape(rows, 3, head_cols)
    return (
        output,
        tokens_grad,
        attn_gain_grad,
        qkv_grad,
        out_grad,
        mlp_gain_grad,
        up_grad,
        down_grad,
    )


def solution(mesh):
    in_specs = (
        P("dp", None),
        P("dp", None),
        P(),
        P("dp", None, "tensor"),
        P("tensor", "dp"),
        P(),
        P("dp", None, "tensor"),
        P("tensor", "dp"),
        P("dp", None),
    )
    out_specs = (
        P("dp", None),
        P("dp", None),
        P("dp"),
        P("dp", None, "tensor"),
        P("tensor", "dp"),
        P("dp"),
        P("dp", None, "tensor"),
        P("tensor", "dp"),
    )
    return jax.shard_map(layer_shards, mesh=mesh, in_specs=in_specs, out_specs=out_specs, check_vma=False)
```

```python
import math

import jax
import jax.numpy as jnp
from jax import lax
from jax.experimental import pallas as pl
from jax.experimental.pallas import tpu as pltpu
from jax.sharding import PartitionSpec as P

HD = 64

eps_norm = 1e-05
theta_base = 160000.0


def row_layout(row_lengths, tok_count):
    doc_ends = jnp.cumsum(row_lengths, dtype=jnp.int32)
    tok_place = jnp.arange(tok_count, dtype=jnp.int32)
    passed = tok_place[:, None] >= doc_ends[None, :]
    segment = jnp.sum(passed.astype(jnp.int32), axis=1, dtype=jnp.int32)
    doc_start = jnp.sum(jnp.where(passed, row_lengths[None, :], 0), axis=1, dtype=jnp.int32)
    return (segment, tok_place - doc_start)


def tile_ranges(row_lengths, tok_count):
    ends = jnp.cumsum(row_lengths, dtype=jnp.int32)
    starts = ends - row_lengths
    begin = jnp.arange(tok_count // TILE, dtype=jnp.int32)[:, None] * TILE
    touched = (ends[None, :] > begin) & (starts[None, :] < begin + TILE)
    low = jnp.min(jnp.where(touched, starts[None, :], tok_count), axis=1)
    high = jnp.max(jnp.where(touched, ends[None, :], 0), axis=1)
    return (low // TILE, (high + TILE - 1) // TILE)


def rotary_tables(position, head_width):
    half_width = head_width // 2
    freq_index = jnp.arange(half_width, dtype=jnp.float32)
    inv_freq = jnp.exp(freq_index * (-2.0 * math.log(theta_base) / head_width))
    angles = inv_freq[:, None] * position.astype(jnp.float32)[None, :]
    cosine, sine = jnp.cos(angles), jnp.sin(angles)
    return jnp.concatenate([cosine, cosine, -sine, sine], axis=0)


def normalize(vector):
    row_mean = jnp.mean(vector, axis=-1, keepdims=True)
    centred = vector - row_mean
    spread = jnp.mean(centred * centred, axis=-1, keepdims=True)
    factor = lax.rsqrt(spread + eps_norm)
    return (centred * factor, factor)


def norm_back(grad_norm_out, normed, factor, gain_vec):
    grad_normed = grad_norm_out * gain_vec
    first_mean = jnp.mean(grad_normed, axis=-1, keepdims=True)
    second_mean = jnp.mean(grad_normed * normed, axis=-1, keepdims=True)
    return factor * (grad_normed - first_mean - normed * second_mean)


TILE = 256
NEG = -1e30


def nt_dot(a, b):
    return lax.dot_general(a, b, (((1,), (1,)), ((), ())), preferred_element_type=jnp.float32)


def nn_dot(a, b):
    return lax.dot_general(a, b, (((1,), (0,)), ((), ())), preferred_element_type=jnp.float32)


def tn_dot(a, b):
    return lax.dot_general(a, b, (((0,), (0,)), ((), ())), preferred_element_type=jnp.float32)


def swap_halves(u):
    half = u.shape[-1] // 2
    return jnp.concatenate([u[:, half:], u[:, :half]], axis=1)


def twice(a):
    return jnp.concatenate([a, a], axis=1)


def lane_fold(op, a):
    return op(a[:, : TILE // 2], a[:, TILE // 2 :])


def whole(shape):
    return pl.BlockSpec(shape, lambda *_: (0,) * len(shape))


def project_heads(h_one, weight, tables, heads):
    tok_count, width = h_one.shape
    cols = heads * HD
    rows = 2 * TILE

    def body(h_ref, w_ref, t_ref, q_ref, k_ref, v_ref):
        full = nn_dot(h_ref[...], w_ref[...])
        turn = jnp.transpose(t_ref[...])
        cosine, sine = turn[:, :HD], turn[:, HD:]
        for h in range(heads):
            u = full[:, h * HD : (h + 1) * HD]
            turned = (u * cosine + swap_halves(u) * sine).astype(jnp.bfloat16)
            q_ref[h] = (turned.astype(jnp.float32) * HD**-0.5).astype(jnp.bfloat16)
            u = full[:, cols + h * HD : cols + (h + 1) * HD]
            k_ref[h] = (u * cosine + swap_halves(u) * sine).astype(jnp.bfloat16)
            v_ref[h] = full[:, 2 * cols + h * HD : 2 * cols + (h + 1) * HD].astype(jnp.bfloat16)

    out = jax.ShapeDtypeStruct((heads, tok_count, HD), jnp.bfloat16)
    return pl.pallas_call(
        body,
        grid=(tok_count // rows,),
        in_specs=[
            pl.BlockSpec((rows, width), lambda i: (i, 0)),
            whole(weight.shape),
            pl.BlockSpec((2 * HD, rows), lambda i: (0, i)),
        ],
        out_specs=[pl.BlockSpec((heads, rows, HD), lambda i: (0, i, 0))] * 3,
        out_shape=[out] * 3,
        name="project_heads",
    )(h_one, weight, tables)


def attend(first, last, place, query, key, value, seg_col, seg_row, parts):
    heads, tok_count, _ = query.shape
    blocks = tok_count // TILE
    share = blocks // parts
    half = TILE // 2

    def body(
        first_ref, last_ref, place_ref, q_ref, k_ref, v_ref, col_ref, row_ref, *refs
    ):
        low_refs, (out_ref, lse_ref, scores, peak, total, accum, low) = refs[:parts], refs[parts:]
        i = pl.program_id(0)
        lo, hi = first_ref[i], last_ref[i]
        peak[...] = jnp.full(peak.shape, NEG, jnp.float32)
        total[...] = jnp.zeros(total.shape, jnp.float32)
        accum[...] = jnp.zeros(accum.shape, jnp.float32)

        def score(j, carry):
            at = pl.multiple_of(j * TILE, TILE)
            same = twice(col_ref[...]) == row_ref[:, pl.ds(at, TILE)]
            for h in range(heads):
                s = jnp.where(same, nt_dot(q_ref[h], k_ref[h, pl.ds(at, TILE), :]), NEG)
                scores[h, j] = s
                peak[h] = jnp.maximum(peak[h], lane_fold(jnp.maximum, s))
            return carry

        lax.fori_loop(lo, hi, score, 0)
        for h in range(heads):
            peak[h] = jnp.broadcast_to(jnp.max(peak[h], axis=1, keepdims=True), (TILE, half))

        def spread(j, carry):
            at = pl.multiple_of(j * TILE, TILE)
            for h in range(heads):
                p = jnp.exp(scores[h, j] - twice(peak[h]))
                total[h] = total[h] + lane_fold(jnp.add, p)
                accum[h] = accum[h] + nn_dot(p.astype(jnp.bfloat16), v_ref[h, pl.ds(at, TILE), :])
            return carry

        lax.fori_loop(lo, hi, spread, 0)
        for h in range(heads):
            norm = jnp.sum(total[h], axis=1, keepdims=True)
            out = accum[h] / norm
            out_ref[h] = out
            low[:, h * HD : (h + 1) * HD] = out.astype(jnp.bfloat16)
            logs = peak[h] + jnp.log(jnp.broadcast_to(norm, (TILE, half)))
            lse_ref[h] = jnp.transpose(logs)[0:1, :]
        rows = pl.ds(pl.multiple_of((i % share) * TILE, TILE), TILE)
        for r in range(parts):

            @pl.when((i // share) ^ place_ref[0] == r)
            def _():
                low_refs[r][rows, :] = low[...]

    tile = pl.BlockSpec((heads, TILE, HD), lambda i, *_: (0, i, 0))
    return pl.pallas_call(
        body,
        grid_spec=pltpu.PrefetchScalarGridSpec(
            num_scalar_prefetch=3,
            grid=(blocks,),
            in_specs=[
                tile,
                whole(key.shape),
                whole(value.shape),
                pl.BlockSpec((TILE, half), lambda i, *_: (i, 0)),
                whole(seg_row.shape),
            ],
            out_specs=[whole((share * TILE, heads * HD))] * parts
            + [
                tile,
                pl.BlockSpec((heads, 1, TILE), lambda i, *_: (0, 0, i)),
            ],
            scratch_shapes=[
                pltpu.VMEM((heads, blocks, TILE, TILE), jnp.float32),
                pltpu.VMEM((heads, TILE, half), jnp.float32),
                pltpu.VMEM((heads, TILE, half), jnp.float32),
                pltpu.VMEM((heads, TILE, HD), jnp.float32),
                pltpu.VMEM((TILE, heads * HD), jnp.bfloat16),
            ],
        ),
        out_shape=[jax.ShapeDtypeStruct((share * TILE, heads * HD), jnp.bfloat16)] * parts
        + [
            jax.ShapeDtypeStruct((heads, tok_count, HD), jnp.float32),
            jax.ShapeDtypeStruct((heads, 1, tok_count), jnp.float32),
        ],
        name="attend",
    )(first, last, place, query, key, value, seg_col, seg_row)


def attend_grad(
    first, last, place, query, key, value, seg_col, seg_row, grads, out, lse, tables
):
    heads, tok_count, _ = query.shape
    blocks = tok_count // TILE
    half = TILE // 2
    cols = heads * HD
    parts = len(grads)
    share = tok_count // parts

    def body(
        first_ref, last_ref, place_ref, q_ref, k_ref, v_ref, col_ref, row_ref, o_ref, lse_ref,
        t_ref, *refs
    ):
        g_refs, (d_ref, split, inner, dq, dk, dv) = refs[:parts], refs[parts:]
        j = pl.program_id(0)
        lo, hi = first_ref[j], last_ref[j]
        here = pl.ds(pl.multiple_of(j * TILE, TILE), TILE)

        @pl.when(j == 0)
        def _():
            dq[...] = jnp.zeros(dq.shape, jnp.float32)
            for b in range(blocks):
                r, off = b * TILE // share, b * TILE % share
                base = (place_ref[0] ^ r) * share + off
                rows = pl.ds(pl.multiple_of(base, TILE), TILE)
                for h in range(heads):
                    g = g_refs[r][off : off + TILE, h * HD : (h + 1) * HD]
                    split[h, rows, :] = g
                    dots = jnp.sum(g.astype(jnp.float32) * o_ref[h, rows, :], axis=1, keepdims=True)
                    dots = jnp.transpose(jnp.broadcast_to(dots, (TILE, half)))
                    inner[h, :, rows] = dots[0:1, :]

        dk[...] = jnp.zeros(dk.shape, jnp.float32)
        dv[...] = jnp.zeros(dv.shape, jnp.float32)

        def step(i, carry):
            at = pl.ds(pl.multiple_of(i * TILE, TILE), TILE)
            same = twice(col_ref[...]) == row_ref[:, at]
            for h in range(heads):
                q, g, k = q_ref[h, at, :], split[h, at, :], k_ref[h, here, :]
                s = jnp.where(same, nt_dot(k, q), NEG)
                p = jnp.exp(s - lse_ref[h, :, at])
                dp = nt_dot(v_ref[h, here, :], g)
                ds = (p * (dp - inner[h, :, at])).astype(jnp.bfloat16)
                dv[h] = dv[h] + nn_dot(p.astype(jnp.bfloat16), g)
                dk[h] = dk[h] + nn_dot(ds, q)
                dq[h, at, :] = dq[h, at, :] + tn_dot(ds, k)
            return carry

        lax.fori_loop(lo, hi, step, 0)
        turn = jnp.transpose(t_ref[:, here])
        cosine, sine = turn[:, :HD], turn[:, HD:]
        for h in range(heads):
            w = dk[h]
            w = (w * cosine - swap_halves(w) * sine).astype(jnp.bfloat16)
            d_ref[here, cols + h * HD : cols + (h + 1) * HD] = w
            d_ref[here, 2 * cols + h * HD : 2 * cols + (h + 1) * HD] = dv[h].astype(jnp.bfloat16)

        @pl.when(j == blocks - 1)
        def _():
            for b in range(blocks):
                rows = slice(b * TILE, (b + 1) * TILE)
                turn = jnp.transpose(t_ref[:, rows])
                cosine, sine = turn[:, :HD], turn[:, HD:]
                for h in range(heads):
                    w = dq[h, rows, :] * HD**-0.5
                    w = w * cosine - swap_halves(w) * sine
                    d_ref[rows, h * HD : (h + 1) * HD] = w.astype(jnp.bfloat16)

    return pl.pallas_call(
        body,
        grid_spec=pltpu.PrefetchScalarGridSpec(
            num_scalar_prefetch=3,
            grid=(blocks,),
            in_specs=[
                whole(query.shape),
                whole(key.shape),
                whole(value.shape),
                pl.BlockSpec((TILE, half), lambda i, *_: (i, 0)),
                whole(seg_row.shape),
                whole(out.shape),
                whole(lse.shape),
                whole(tables.shape),
            ]
            + [whole(g.shape) for g in grads],
            out_specs=whole((tok_count, 3 * cols)),
            scratch_shapes=[
                pltpu.VMEM((heads, tok_count, HD), jnp.bfloat16),
                pltpu.VMEM((heads, 1, tok_count), jnp.float32),
                pltpu.VMEM((heads, tok_count, HD), jnp.float32),
                pltpu.VMEM((heads, TILE, HD), jnp.float32),
                pltpu.VMEM((heads, TILE, HD), jnp.float32),
            ],
        ),
        out_shape=jax.ShapeDtypeStruct((tok_count, 3 * cols), jnp.bfloat16),
        name="attend_grad",
    )(first, last, place, query, key, value, seg_col, seg_row, out, lse, tables, *grads)


def swap(value, axis, step):
    count = lax.axis_size(axis)
    return lax.ppermute(value, axis, [(i, i ^ step) for i in range(count)])


def gather_far(shard):
    return [shard] + [swap(shard, "dp", step) for step in range(2, lax.axis_size("dp"), 2)]


def gather_near(pieces):
    return [v for piece in pieces for v in (piece, swap(piece, "dp", 1))]


def assemble(pieces, place, kind=None):
    count = len(pieces)
    lead, (rows, cols) = pieces[0].shape[:-2], pieces[0].shape[-2:]
    if rows % 16:
        order = place[0] ^ jnp.arange(count, dtype=jnp.int32)
        ranked = jnp.take(jnp.stack(pieces), order, axis=0, mode="clip")
        return jnp.moveaxis(ranked, 0, -3).reshape(*lead, count * rows, cols)

    kind = kind or pieces[0].dtype

    def body(place_ref, *refs):
        for r in range(count):
            at = pl.ds(pl.multiple_of((place_ref[0] ^ r) * rows, 16), rows)
            refs[count][(slice(None),) * len(lead) + (at, slice(None))] = refs[r][...].astype(kind)

    return pl.pallas_call(
        body,
        grid_spec=pltpu.PrefetchScalarGridSpec(
            num_scalar_prefetch=1,
            grid=(1,),
            in_specs=[whole(pieces[0].shape)] * count,
            out_specs=whole((*lead, count * rows, cols)),
        ),
        out_shape=jax.ShapeDtypeStruct((*lead, count * rows, cols), kind),
        name="assemble",
    )(place, *pieces)


def reduce_near(total, place):
    count = lax.axis_size("dp")
    rows, cols = total.shape[0] // count, total.shape[1]
    order = place[0] ^ jnp.array([*range(0, count, 2), *range(1, count, 2)], jnp.int32)
    ranked = jnp.take(total.reshape(count, rows, cols), order, axis=0, mode="clip")
    return ranked[: count // 2], swap(ranked[count // 2 :], "dp", 1)


def reduce_far(near, come):
    near = near.astype(jnp.float32) + come.astype(jnp.float32)
    low = near.astype(jnp.bfloat16)
    result = near[0]
    for slot in range(1, near.shape[0]):
        result = result + swap(low[slot], "dp", 2 * slot).astype(jnp.float32)
    return result


def layer(
    att, source, cot, gain, weight_near, weight_far, hid
):
    tok_count, width = source.shape
    head_cols = att[0].shape[1]
    parts = len(att)
    ff = parts * hid
    inner = parts * head_cols
    rows = 256

    def body(*refs):
        a_refs = refs[:parts]
        x_ref, c_ref, g_ref, wa_ref, wb_ref = refs[parts : parts + 5]
        out_ref, dmid_ref, dlow_ref, h_ref, hid_ref, dg_ref, dv_ref, gg_ref = refs[
            parts + 5 : parts + 13
        ]
        d_refs = refs[parts + 13 : 2 * parts + 13]
        gate, lift, down, proj = refs[2 * parts + 13 :]

        @pl.when(pl.program_id(0) == 0)
        def _():
            gg_ref[...] = jnp.zeros(gg_ref.shape, jnp.float32)
            for slot in range(parts):
                w_ref, s = (wa_ref, wb_ref)[slot // 2], slot % 2
                at = slice(slot * hid, (slot + 1) * hid)
                gate[:, at] = w_ref[s, :, :hid]
                lift[:, at] = w_ref[s, :, hid : 2 * hid]
                down[:, at] = w_ref[s, :, 2 * hid : 3 * hid]
                proj[:, slot * head_cols : (slot + 1) * head_cols] = w_ref[
                    s, :, 3 * hid : 3 * hid + head_cols
                ]

        gain_vec = g_ref[...]
        attended = jnp.concatenate([a_refs[r][...] for r in SLOTS], axis=1)
        mid = x_ref[...].astype(jnp.float32) + nt_dot(attended, proj[...])
        normed, factor = normalize(mid)
        h_two = (normed * gain_vec).astype(jnp.bfloat16)
        h_ref[...] = h_two
        cot_low = c_ref[...]
        first = nn_dot(h_two, gate[...])
        second = nn_dot(h_two, lift[...])
        below = 0.5 * (1.0 + lax.erf(first * math.sqrt(0.5)))
        active = first * below
        hidden = (active * second).astype(jnp.bfloat16)
        hid_ref[...] = hidden
        out_ref[...] = (mid + nt_dot(hidden, down[...])).astype(jnp.bfloat16)
        slope = below + first * (jnp.exp(-0.5 * first * first) * (1.0 / math.sqrt(2.0 * math.pi)))
        d_hidden = nn_dot(cot_low, down[...]).astype(jnp.bfloat16).astype(jnp.float32)
        d_first = (d_hidden * second * slope).astype(jnp.bfloat16)
        d_second = (d_hidden * active).astype(jnp.bfloat16)
        dg_ref[...] = d_first
        dv_ref[...] = d_second
        d_h = nt_dot(d_first, gate[...]) + nt_dot(d_second, lift[...])
        gg_ref[...] += jnp.sum(d_h * normed, axis=0, keepdims=True)
        d_mid = cot_low.astype(jnp.float32) + norm_back(d_h, normed, factor, gain_vec)
        dmid_ref[...] = d_mid
        d_low = d_mid.astype(jnp.bfloat16)
        dlow_ref[...] = d_low
        d_att = nn_dot(d_low, proj[...]).astype(jnp.bfloat16)
        for slot in range(parts):
            d_refs[SLOTS[slot]][...] = d_att[:, slot * head_cols : (slot + 1) * head_cols]

    def tile(cols):
        return pl.BlockSpec((rows, cols), lambda i: (i, 0))

    def fixed(shape):
        return pl.BlockSpec(shape, lambda *_: (0,) * len(shape), pipeline_mode=pl.Buffered(1))

    def shape(cols, kind=jnp.bfloat16):
        return jax.ShapeDtypeStruct((tok_count, cols), kind)

    return pl.pallas_call(
        body,
        grid=(tok_count // rows,),
        in_specs=[tile(head_cols)] * parts
        + [tile(width), tile(width), whole((1, width))]
        + [fixed(weight_near.shape), fixed(weight_far.shape)],
        out_specs=[tile(width)] * 4
        + [tile(ff)] * 3
        + [whole((1, width))]
        + [tile(head_cols)] * parts,
        out_shape=[
            shape(width),
            shape(width, jnp.float32),
            shape(width),
            shape(width),
            shape(ff),
            shape(ff),
            shape(ff),
            jax.ShapeDtypeStruct((1, width), jnp.float32),
        ]
        + [shape(head_cols)] * parts,
        scratch_shapes=[
            pltpu.VMEM((width, ff), jnp.bfloat16),
            pltpu.VMEM((width, ff), jnp.bfloat16),
            pltpu.VMEM((width, ff), jnp.bfloat16),
            pltpu.VMEM((width, inner), jnp.bfloat16),
        ],
        name="layer",
    )(*att, source, cot, gain[None, :], weight_near, weight_far)


SLOTS = (0, 2, 1, 3)


def weight_grads(side, h_two, d_first, d_second, cot, hidden, d_low, att, gain_grad, wide):
    _, width = h_two.shape
    hid = hidden.shape[1] // len(SLOTS)
    head_cols = att[0].shape[1]
    both = tuple(att[r] for r in SLOTS[2 * side : 2 * side + 2])
    here = slice(2 * side * hid, (2 * side + 2) * hid)

    def body(h_ref, f_ref, s_ref, c_ref, u_ref, l_ref, a_ref, b_ref, g_ref, out_ref):
        sides = jnp.concatenate([f_ref[:, here], s_ref[:, here]], axis=1)
        full = tn_dot(h_ref[...], sides).astype(jnp.bfloat16)
        for s in range(2):
            out_ref[s, :, :hid] = full[:, s * hid : (s + 1) * hid]
            out_ref[s, :, hid : 2 * hid] = full[:, (2 + s) * hid : (3 + s) * hid]
        full = tn_dot(c_ref[...], u_ref[:, here]).astype(jnp.bfloat16)
        heads = tn_dot(l_ref[...], jnp.concatenate([a_ref[...], b_ref[...]], axis=1))
        heads = heads.astype(jnp.bfloat16)
        gain_col = jnp.transpose(jnp.broadcast_to(g_ref[...], (128, width))).astype(jnp.bfloat16)
        at = 3 * hid
        for s in range(2):
            out_ref[s, :, 2 * hid : at] = full[:, s * hid : (s + 1) * hid]
            out_ref[s, :, at : at + head_cols] = heads[:, s * head_cols : (s + 1) * head_cols]
            out_ref[s, :, at + head_cols :] = gain_col[:, : wide - at - head_cols]

    return pl.pallas_call(
        body,
        out_shape=jax.ShapeDtypeStruct((2, width, wide), jnp.bfloat16),
        name="weight_grads",
    )(h_two, d_first, d_second, cot, hidden, d_low, *both, gain_grad)


def back_to_width(d_qkv, weight, place, slots, share):
    width, cols = weight.shape
    first, stride = slots[0], slots[1] - slots[0]

    def body(place_ref, d_ref, w_ref, out_ref):
        out_ref[0] = nt_dot(d_ref[...], w_ref[...]).astype(jnp.bfloat16)

    return pl.pallas_call(
        body,
        grid_spec=pltpu.PrefetchScalarGridSpec(
            num_scalar_prefetch=1,
            grid=(len(slots),),
            in_specs=[
                pl.BlockSpec((share, cols), lambda i, at: (at[0] ^ (first + stride * i), 0)),
                whole(weight.shape),
            ],
            out_specs=pl.BlockSpec((1, share, width), lambda i, at: (i, 0, 0)),
        ),
        out_shape=jax.ShapeDtypeStruct((len(slots), share, width), jnp.bfloat16),
        name="back_to_width",
    )(place, d_qkv, weight)


def share_rows(mine, place, kind=None):
    other = swap(mine, "tensor", 2)
    beside = swap(mine, "tensor", 1)
    across = swap(other, "tensor", 1)
    return assemble([mine, beside, other, across], place, kind)


def layer_shards(
    tokens, lengths, attn_gain, qkv_weight, out_weight, mlp_gain, up_weight, down_weight, cotangent
):
    tok_count, _ = tokens.shape
    parts = lax.axis_size("tensor")
    share = tok_count // parts
    rank = lax.axis_index("tensor").astype(jnp.int32)
    place = rank[None]
    dp_place = lax.axis_index("dp").astype(jnp.int32)[None]
    rows = qkv_weight.shape[0]
    head_cols = qkv_weight.shape[2]
    heads_dev = head_cols // HD
    hid = up_weight.shape[2]
    used = 3 * hid + head_cols
    wide = used // 128 * 128 + 128

    qkv_own = qkv_weight.reshape(rows, 3 * head_cols)
    qkv_own, up_weight, down_weight, out_weight = lax.optimization_barrier(
        (qkv_own, up_weight, down_weight, out_weight)
    )
    qkv_far = gather_far(qkv_own)
    qkv_flat = assemble(gather_near(qkv_far), dp_place)
    packed = jnp.concatenate(
        [
            up_weight.reshape(rows, 2 * hid),
            down_weight.T,
            out_weight.T,
            jnp.zeros((rows, wide - used), jnp.bfloat16),
        ],
        axis=1,
    )
    paired = jnp.stack([packed, swap(packed, "tensor", 2)])
    paired, _ = lax.optimization_barrier((paired, qkv_far))
    paired_far = gather_far(paired)

    segment, position = row_layout(lengths[0], tok_count)
    tables = rotary_tables(position, HD)
    h_one = (normalize(tokens.astype(jnp.float32))[0] * attn_gain).astype(jnp.bfloat16)
    seg_col = jnp.broadcast_to(segment[:, None], (tok_count, TILE // 2))
    seg_row = segment[None, :]
    first, last = tile_ranges(lengths[0], tok_count)
    query, key, value = project_heads(h_one, qkv_flat, tables, heads_dev)
    paired_far, query = lax.optimization_barrier((paired_far, query))
    pieces = gather_near(paired_far)
    *sent, attended_wide, log_total = attend(
        first, last, place, query, key, value, seg_col, seg_row, parts
    )
    weight_near = assemble(pieces, dp_place)
    weight_far = swap(weight_near, "tensor", 1)
    att = [sent[0]] + [swap(sent[r], "tensor", r) for r in range(1, parts)]
    my_tokens = lax.dynamic_slice_in_dim(tokens, rank * share, share, 0)
    my_cot = lax.dynamic_slice_in_dim(cotangent, rank * share, share, 0)
    out, d_mid, d_low, h_two, hidden, d_first, d_second, gain_two, *d_sent = layer(
        att, my_tokens, my_cot, mlp_gain, weight_near, weight_far, hid
    )
    d_att = [d_sent[0]] + [swap(d_sent[r], "tensor", r) for r in range(1, parts)]
    output = share_rows(out, place)

    grads_in = (h_two, d_first, d_second, my_cot, hidden, d_low, att, gain_two, wide)
    grads_far = weight_grads(1, *grads_in)
    grads_near = weight_grads(0, *grads_in)
    grads_come = swap(grads_far, "tensor", 1)
    chip_sent = grads_near[1].astype(jnp.float32) + grads_come[1].astype(jnp.float32)
    chip_sent, d_att = lax.optimization_barrier((chip_sent.astype(jnp.bfloat16), d_att))
    column_come = swap(chip_sent, "tensor", 2)

    d_qkv = attend_grad(
        first,
        last,
        place,
        query,
        key,
        value,
        seg_col,
        seg_row,
        d_att,
        attended_wide,
        log_total,
        tables,
    )
    d_far = back_to_width(d_qkv, qkv_flat, place, (1, 3), share)
    d_near = back_to_width(d_qkv, qkv_flat, place, (0, 2), share)
    d_side = swap(d_far, "tensor", 1)
    d_sent = d_near[1].astype(jnp.float32) + d_side[1].astype(jnp.float32)
    d_sent, d_qkv, column_come = lax.optimization_barrier(
        (d_sent.astype(jnp.bfloat16), d_qkv, column_come)
    )
    d_come = swap(d_sent, "tensor", 2)
    column = grads_near[0].astype(jnp.float32) + grads_come[0].astype(jnp.float32)
    column = (column + column_come.astype(jnp.float32)).astype(jnp.bfloat16)
    column_near, column_come = reduce_near(column, dp_place)
    qkv_total = jnp.einsum("td,tf->df", h_one, d_qkv, preferred_element_type=jnp.float32)
    qkv_near, qkv_come = reduce_near(qkv_total.astype(jnp.bfloat16), dp_place)
    normed_one, factor_one = normalize(my_tokens.astype(jnp.float32))
    d_h_one = d_near[0].astype(jnp.float32) + d_side[0].astype(jnp.float32)
    d_h_one = d_h_one + d_come.astype(jnp.float32)
    tokens_grad = d_mid + norm_back(d_h_one, normed_one, factor_one, attn_gain)
    tokens_grad = share_rows(tokens_grad.astype(jnp.bfloat16), place, jnp.float32)
    reduced = reduce_far(column_near, column_come)
    up_grad = reduced[:, : 2 * hid].reshape(rows, 2, hid)
    down_grad = reduced[:, 2 * hid : 3 * hid].T
    out_grad = reduced[:, 3 * hid : used].T
    mlp_gain_grad = reduced[:, used]
    qkv_grad = reduce_far(qkv_near, qkv_come)
    gain_one = jnp.sum(qkv_grad * qkv_own.astype(jnp.float32), axis=1)
    gain_one = gain_one + sum(swap(gain_one, "tensor", r) for r in range(1, parts))
    attn_gain_grad = gain_one / lax.dynamic_slice_in_dim(attn_gain, dp_place[0] * rows, rows, 0)
    qkv_grad = qkv_grad.reshape(rows, 3, head_cols)
    return (
        output,
        tokens_grad,
        attn_gain_grad,
        qkv_grad,
        out_grad,
        mlp_gain_grad,
        up_grad,
        down_grad,
    )


def solution(mesh):
    in_specs = (
        P("dp", None),
        P("dp", None),
        P(),
        P("dp", None, "tensor"),
        P("tensor", "dp"),
        P(),
        P("dp", None, "tensor"),
        P("tensor", "dp"),
        P("dp", None),
    )
    out_specs = (
        P("dp", None),
        P("dp", None),
        P("dp"),
        P("dp", None, "tensor"),
        P("tensor", "dp"),
        P("dp"),
        P("dp", None, "tensor"),
        P("tensor", "dp"),
    )
    return jax.shard_map(layer_shards, mesh=mesh, in_specs=in_specs, out_specs=out_specs, check_vma=False)
```

```python
import math

import jax
import jax.numpy as jnp
from jax import lax
from jax.experimental import pallas as pl
from jax.experimental.pallas import tpu as pltpu
from jax.sharding import PartitionSpec as P

HD = 64

eps_norm = 1e-05
theta_base = 160000.0


def row_layout(row_lengths, tok_count):
    doc_ends = jnp.cumsum(row_lengths, dtype=jnp.int32)
    tok_place = jnp.arange(tok_count, dtype=jnp.int32)
    passed = tok_place[:, None] >= doc_ends[None, :]
    segment = jnp.sum(passed.astype(jnp.int32), axis=1, dtype=jnp.int32)
    doc_start = jnp.sum(jnp.where(passed, row_lengths[None, :], 0), axis=1, dtype=jnp.int32)
    return (segment, tok_place - doc_start)


def tile_ranges(row_lengths, tok_count):
    ends = jnp.cumsum(row_lengths, dtype=jnp.int32)
    starts = ends - row_lengths
    begin = jnp.arange(tok_count // TILE, dtype=jnp.int32)[:, None] * TILE
    touched = (ends[None, :] > begin) & (starts[None, :] < begin + TILE)
    low = jnp.min(jnp.where(touched, starts[None, :], tok_count), axis=1)
    high = jnp.max(jnp.where(touched, ends[None, :], 0), axis=1)
    return (low // TILE, (high + TILE - 1) // TILE)


def rotary_tables(position, head_width):
    half_width = head_width // 2
    freq_index = jnp.arange(half_width, dtype=jnp.float32)
    inv_freq = jnp.exp(freq_index * (-2.0 * math.log(theta_base) / head_width))
    angles = inv_freq[:, None] * position.astype(jnp.float32)[None, :]
    cosine, sine = jnp.cos(angles), jnp.sin(angles)
    return jnp.concatenate([cosine, cosine, -sine, sine], axis=0)


def normalize(vector):
    row_mean = jnp.mean(vector, axis=-1, keepdims=True)
    centred = vector - row_mean
    spread = jnp.mean(centred * centred, axis=-1, keepdims=True)
    factor = lax.rsqrt(spread + eps_norm)
    return (centred * factor, factor)


def norm_back(grad_norm_out, normed, factor, gain_vec):
    grad_normed = grad_norm_out * gain_vec
    first_mean = jnp.mean(grad_normed, axis=-1, keepdims=True)
    second_mean = jnp.mean(grad_normed * normed, axis=-1, keepdims=True)
    return factor * (grad_normed - first_mean - normed * second_mean)


TILE = 256
NEG = -1e30


def nt_dot(a, b):
    return lax.dot_general(a, b, (((1,), (1,)), ((), ())), preferred_element_type=jnp.float32)


def nn_dot(a, b):
    return lax.dot_general(a, b, (((1,), (0,)), ((), ())), preferred_element_type=jnp.float32)


def tn_dot(a, b):
    return lax.dot_general(a, b, (((0,), (0,)), ((), ())), preferred_element_type=jnp.float32)


def swap_halves(u):
    half = u.shape[-1] // 2
    return jnp.concatenate([u[:, half:], u[:, :half]], axis=1)


def twice(a):
    return jnp.concatenate([a, a], axis=1)


def lane_fold(op, a):
    return op(a[:, : TILE // 2], a[:, TILE // 2 :])


def whole(shape):
    return pl.BlockSpec(shape, lambda *_: (0,) * len(shape))


def project_heads(h_one, weight, tables, heads):
    tok_count, width = h_one.shape
    cols = heads * HD
    rows = 2 * TILE

    def body(h_ref, w_ref, t_ref, q_ref, k_ref, v_ref):
        full = nn_dot(h_ref[...], w_ref[...])
        turn = jnp.transpose(t_ref[...])
        cosine, sine = turn[:, :HD], turn[:, HD:]
        for h in range(heads):
            u = full[:, h * HD : (h + 1) * HD]
            turned = (u * cosine + swap_halves(u) * sine).astype(jnp.bfloat16)
            q_ref[h] = (turned.astype(jnp.float32) * HD**-0.5).astype(jnp.bfloat16)
            u = full[:, cols + h * HD : cols + (h + 1) * HD]
            k_ref[h] = (u * cosine + swap_halves(u) * sine).astype(jnp.bfloat16)
            v_ref[h] = full[:, 2 * cols + h * HD : 2 * cols + (h + 1) * HD].astype(jnp.bfloat16)

    out = jax.ShapeDtypeStruct((heads, tok_count, HD), jnp.bfloat16)
    return pl.pallas_call(
        body,
        grid=(tok_count // rows,),
        in_specs=[
            pl.BlockSpec((rows, width), lambda i: (i, 0)),
            whole(weight.shape),
            pl.BlockSpec((2 * HD, rows), lambda i: (0, i)),
        ],
        out_specs=[pl.BlockSpec((heads, rows, HD), lambda i: (0, i, 0))] * 3,
        out_shape=[out] * 3,
        name="project_heads",
    )(h_one, weight, tables)


def attend(first, last, place, query, key, value, seg_col, seg_row, parts):
    heads, tok_count, _ = query.shape
    blocks = tok_count // TILE
    share = blocks // parts
    half = TILE // 2

    def body(
        first_ref, last_ref, place_ref, q_ref, k_ref, v_ref, col_ref, row_ref, *refs
    ):
        low_refs, (out_ref, lse_ref, scores, peak, total, accum, low) = refs[:parts], refs[parts:]
        i = pl.program_id(0)
        lo, hi = first_ref[i], last_ref[i]
        peak[...] = jnp.full(peak.shape, NEG, jnp.float32)
        total[...] = jnp.zeros(total.shape, jnp.float32)
        accum[...] = jnp.zeros(accum.shape, jnp.float32)

        def score(j, carry):
            at = pl.multiple_of(j * TILE, TILE)
            same = twice(col_ref[...]) == row_ref[:, pl.ds(at, TILE)]
            for h in range(heads):
                s = jnp.where(same, nt_dot(q_ref[h], k_ref[h, pl.ds(at, TILE), :]), NEG)
                scores[h, j] = s
                peak[h] = jnp.maximum(peak[h], lane_fold(jnp.maximum, s))
            return carry

        lax.fori_loop(lo, hi, score, 0)
        for h in range(heads):
            peak[h] = jnp.broadcast_to(jnp.max(peak[h], axis=1, keepdims=True), (TILE, half))

        def spread(j, carry):
            at = pl.multiple_of(j * TILE, TILE)
            for h in range(heads):
                p = jnp.exp(scores[h, j] - twice(peak[h]))
                total[h] = total[h] + lane_fold(jnp.add, p)
                accum[h] = accum[h] + nn_dot(p.astype(jnp.bfloat16), v_ref[h, pl.ds(at, TILE), :])
            return carry

        lax.fori_loop(lo, hi, spread, 0)
        lane = lax.broadcasted_iota(jnp.int32, (TILE, half), 1)
        norms, peaks = jnp.ones((TILE, half), jnp.float32), peak[0]
        for h in range(heads):
            norm = jnp.sum(total[h], axis=1, keepdims=True)
            norms = jnp.where(lane == h, norm, norms)
            peaks = jnp.where(lane == h, peak[h], peaks)
            out = accum[h] / norm
            out_ref[h] = out
            low[:, h * HD : (h + 1) * HD] = out.astype(jnp.bfloat16)
        logs = jnp.transpose(peaks + jnp.log(norms))
        for h in range(heads):
            lse_ref[h] = logs[h : h + 1, :]
        rows = pl.ds(pl.multiple_of((i % share) * TILE, TILE), TILE)
        for r in range(parts):

            @pl.when((i // share) ^ place_ref[0] == r)
            def _():
                low_refs[r][rows, :] = low[...]

    tile = pl.BlockSpec((heads, TILE, HD), lambda i, *_: (0, i, 0))
    return pl.pallas_call(
        body,
        grid_spec=pltpu.PrefetchScalarGridSpec(
            num_scalar_prefetch=3,
            grid=(blocks,),
            in_specs=[
                tile,
                whole(key.shape),
                whole(value.shape),
                pl.BlockSpec((TILE, half), lambda i, *_: (i, 0)),
                whole(seg_row.shape),
            ],
            out_specs=[whole((share * TILE, heads * HD))] * parts
            + [
                tile,
                pl.BlockSpec((heads, 1, TILE), lambda i, *_: (0, 0, i)),
            ],
            scratch_shapes=[
                pltpu.VMEM((heads, blocks, TILE, TILE), jnp.float32),
                pltpu.VMEM((heads, TILE, half), jnp.float32),
                pltpu.VMEM((heads, TILE, half), jnp.float32),
                pltpu.VMEM((heads, TILE, HD), jnp.float32),
                pltpu.VMEM((TILE, heads * HD), jnp.bfloat16),
            ],
        ),
        out_shape=[jax.ShapeDtypeStruct((share * TILE, heads * HD), jnp.bfloat16)] * parts
        + [
            jax.ShapeDtypeStruct((heads, tok_count, HD), jnp.float32),
            jax.ShapeDtypeStruct((heads, 1, tok_count), jnp.float32),
        ],
        name="attend",
    )(first, last, place, query, key, value, seg_col, seg_row)


def attend_grad(
    first, last, place, query, key, value, seg_col, seg_row, grads, out, lse, tables, head, done
):
    all_heads, tok_count, _ = query.shape
    heads = all_heads - 1 if head == 0 else 1
    blocks = tok_count // TILE
    half = TILE // 2
    cols = all_heads * HD
    parts = len(grads)
    share = tok_count // parts

    def body(
        first_ref, last_ref, place_ref, q_ref, k_ref, v_ref, col_ref, row_ref, o_ref, lse_ref,
        t_ref, *refs
    ):
        g_refs, done_refs = refs[:parts], refs[parts:-6]
        d_ref, split, inner, dq, dk, dv = refs[-6:]
        j = pl.program_id(0)
        lo, hi = first_ref[j], last_ref[j]
        here = pl.ds(pl.multiple_of(j * TILE, TILE), TILE)

        @pl.when(j == 0)
        def _():
            dq[...] = jnp.zeros(dq.shape, jnp.float32)
            for ref in done_refs:
                d_ref[...] = ref[...]
            lane = lax.broadcasted_iota(jnp.int32, (TILE, half), 1)
            for b in range(blocks):
                r, off = b * TILE // share, b * TILE % share
                base = (place_ref[0] ^ r) * share + off
                rows = pl.ds(pl.multiple_of(base, TILE), TILE)
                sums = jnp.zeros((TILE, half), jnp.float32)
                for h in range(heads):
                    at = (head + h) * HD
                    g = g_refs[r][off : off + TILE, at : at + HD]
                    split[h, rows, :] = g
                    dots = jnp.sum(g.astype(jnp.float32) * o_ref[h, rows, :], axis=1, keepdims=True)
                    sums = jnp.where(lane == h, dots, sums)
                sums = jnp.transpose(sums)
                for h in range(heads):
                    inner[h, :, rows] = sums[h : h + 1, :]

        dk[...] = jnp.zeros(dk.shape, jnp.float32)
        dv[...] = jnp.zeros(dv.shape, jnp.float32)

        def step(i, carry):
            at = pl.ds(pl.multiple_of(i * TILE, TILE), TILE)
            same = twice(col_ref[...]) == row_ref[:, at]
            for h in range(heads):
                q, g, k = q_ref[h, at, :], split[h, at, :], k_ref[h, here, :]
                s = jnp.where(same, nt_dot(k, q), NEG)
                p = jnp.exp(s - lse_ref[h, :, at])
                dp = nt_dot(v_ref[h, here, :], g)
                ds = (p * (dp - inner[h, :, at])).astype(jnp.bfloat16)
                dv[h] = dv[h] + nn_dot(p.astype(jnp.bfloat16), g)
                dk[h] = dk[h] + nn_dot(ds, q)
                dq[h, at, :] = dq[h, at, :] + tn_dot(ds, k)
            return carry

        lax.fori_loop(lo, hi, step, 0)
        source = lax.broadcasted_iota(jnp.int32, (HD, HD), 0)
        target = lax.broadcasted_iota(jnp.int32, (HD, HD), 1)
        moves = (source == (target + HD // 2) % HD).astype(jnp.float32).astype(jnp.bfloat16)
        turn = jnp.transpose(t_ref[:, here])
        cosine, sine = turn[:, :HD], turn[:, HD:]
        for h in range(heads):
            at = cols + (head + h) * HD
            w = dk[h]
            w = w * cosine - nn_dot(w.astype(jnp.bfloat16), moves) * sine
            d_ref[here, at : at + HD] = w.astype(jnp.bfloat16)
            d_ref[here, cols + at : cols + at + HD] = dv[h].astype(jnp.bfloat16)

        @pl.when(j == blocks - 1)
        def _():
            for b in range(blocks):
                rows = slice(b * TILE, (b + 1) * TILE)
                turn = jnp.transpose(t_ref[:, rows])
                cosine, sine = turn[:, :HD], turn[:, HD:]
                for h in range(heads):
                    w = dq[h, rows, :] * HD**-0.5
                    w = w * cosine - nn_dot(w.astype(jnp.bfloat16), moves) * sine
                    at = (head + h) * HD
                    d_ref[rows, at : at + HD] = w.astype(jnp.bfloat16)

    some = pl.BlockSpec((heads, tok_count, HD), lambda *_: (head // heads, 0, 0))
    return pl.pallas_call(
        body,
        grid_spec=pltpu.PrefetchScalarGridSpec(
            num_scalar_prefetch=3,
            grid=(blocks,),
            in_specs=[
                some,
                some,
                some,
                pl.BlockSpec((TILE, half), lambda i, *_: (i, 0)),
                whole(seg_row.shape),
                some,
                pl.BlockSpec((heads, 1, tok_count), lambda *_: (head // heads, 0, 0)),
                whole(tables.shape),
            ]
            + [whole(g.shape) for g in (*grads, *done)],
            out_specs=whole((tok_count, 3 * cols)),
            scratch_shapes=[
                pltpu.VMEM((heads, tok_count, HD), jnp.bfloat16),
                pltpu.VMEM((heads, 1, tok_count), jnp.float32),
                pltpu.VMEM((heads, tok_count, HD), jnp.float32),
                pltpu.VMEM((heads, TILE, HD), jnp.float32),
                pltpu.VMEM((heads, TILE, HD), jnp.float32),
            ],
        ),
        out_shape=jax.ShapeDtypeStruct((tok_count, 3 * cols), jnp.bfloat16),
        name="attend_grad",
    )(first, last, place, query, key, value, seg_col, seg_row, out, lse, tables, *grads, *done)


def swap(value, axis, step):
    count = lax.axis_size(axis)
    return lax.ppermute(value, axis, [(i, i ^ step) for i in range(count)])


def gather_far(shard):
    return [shard] + [swap(shard, "dp", step) for step in range(2, lax.axis_size("dp"), 2)]


def gather_near(pieces):
    return [v for piece in pieces for v in (piece, swap(piece, "dp", 1))]


def assemble(pieces, place, kind=None):
    count = len(pieces)
    lead, (rows, cols) = pieces[0].shape[:-2], pieces[0].shape[-2:]
    if rows % 16:
        order = place[0] ^ jnp.arange(count, dtype=jnp.int32)
        ranked = jnp.take(jnp.stack(pieces), order, axis=0, mode="clip")
        return jnp.moveaxis(ranked, 0, -3).reshape(*lead, count * rows, cols)

    kind = kind or pieces[0].dtype

    def body(place_ref, *refs):
        for r in range(count):
            at = pl.ds(pl.multiple_of((place_ref[0] ^ r) * rows, 16), rows)
            refs[count][(slice(None),) * len(lead) + (at, slice(None))] = refs[r][...].astype(kind)

    return pl.pallas_call(
        body,
        grid_spec=pltpu.PrefetchScalarGridSpec(
            num_scalar_prefetch=1,
            grid=(1,),
            in_specs=[whole(pieces[0].shape)] * count,
            out_specs=whole((*lead, count * rows, cols)),
        ),
        out_shape=jax.ShapeDtypeStruct((*lead, count * rows, cols), kind),
        name="assemble",
    )(place, *pieces)


def reduce_near(total, place):
    count = lax.axis_size("dp")
    blocks = total.reshape(count, total.shape[0] // count, total.shape[1])
    near, far = (
        jnp.take(blocks, place[0] ^ jnp.arange(k, count, 2), axis=0, mode="clip") for k in (0, 1)
    )
    return near, swap(far, "dp", 1)


def reduce_far(near, come):
    near = near.astype(jnp.float32) + come.astype(jnp.float32)
    low = near.astype(jnp.bfloat16)
    come = [swap(low[slot], "dp", 2 * slot) for slot in range(1, near.shape[0])]
    return near[0] + sum(part.astype(jnp.float32) for part in come)


def layer(
    att, source, cot, gain, weight_near, weight_far, hid
):
    tok_count, width = source.shape
    head_cols = att[0].shape[1]
    parts = len(att)
    ff = parts * hid
    inner = parts * head_cols
    rows = 256

    def body(*refs):
        a_refs = refs[:parts]
        x_ref, c_ref, g_ref, wa_ref, wb_ref = refs[parts : parts + 5]
        out_ref, dmid_ref, dlow_ref, h_ref, hid_ref, dg_ref, dv_ref, gg_ref = refs[
            parts + 5 : parts + 13
        ]
        d_refs = refs[parts + 13 : 2 * parts + 13]
        gate, lift, down, proj = refs[2 * parts + 13 :]

        @pl.when(pl.program_id(0) == 0)
        def _():
            gg_ref[...] = jnp.zeros(gg_ref.shape, jnp.float32)
            for slot in range(parts):
                w_ref, s = (wa_ref, wb_ref)[slot // 2], slot % 2
                at = slice(slot * hid, (slot + 1) * hid)
                gate[:, at] = w_ref[s, :, :hid]
                lift[:, at] = w_ref[s, :, hid : 2 * hid]
                down[:, at] = w_ref[s, :, 2 * hid : 3 * hid]
                proj[:, slot * head_cols : (slot + 1) * head_cols] = w_ref[
                    s, :, 3 * hid : 3 * hid + head_cols
                ]

        gain_vec = g_ref[...]
        attended = jnp.concatenate([a_refs[r][...] for r in SLOTS], axis=1)
        mid = x_ref[...].astype(jnp.float32) + nt_dot(attended, proj[...])
        normed, factor = normalize(mid)
        h_two = (normed * gain_vec).astype(jnp.bfloat16)
        h_ref[...] = h_two
        cot_low = c_ref[...]
        first = nn_dot(h_two, gate[...])
        second = nn_dot(h_two, lift[...])
        below = 0.5 * (1.0 + lax.erf(first * math.sqrt(0.5)))
        active = first * below
        hidden = (active * second).astype(jnp.bfloat16)
        hid_ref[...] = hidden
        out_ref[...] = (mid + nt_dot(hidden, down[...])).astype(jnp.bfloat16)
        slope = below + first * (jnp.exp(-0.5 * first * first) * (1.0 / math.sqrt(2.0 * math.pi)))
        d_hidden = nn_dot(cot_low, down[...]).astype(jnp.bfloat16).astype(jnp.float32)
        d_first = (d_hidden * second * slope).astype(jnp.bfloat16)
        d_second = (d_hidden * active).astype(jnp.bfloat16)
        dg_ref[...] = d_first
        dv_ref[...] = d_second
        d_h = nt_dot(d_first, gate[...]) + nt_dot(d_second, lift[...])
        gg_ref[...] += jnp.sum(d_h * normed, axis=0, keepdims=True)
        d_mid = cot_low.astype(jnp.float32) + norm_back(d_h, normed, factor, gain_vec)
        dmid_ref[...] = d_mid
        d_low = d_mid.astype(jnp.bfloat16)
        dlow_ref[...] = d_low
        d_att = nn_dot(d_low, proj[...]).astype(jnp.bfloat16)
        for slot in range(parts):
            d_refs[SLOTS[slot]][...] = d_att[:, slot * head_cols : (slot + 1) * head_cols]

    def tile(cols):
        return pl.BlockSpec((rows, cols), lambda i: (i, 0))

    def fixed(shape):
        return pl.BlockSpec(shape, lambda *_: (0,) * len(shape), pipeline_mode=pl.Buffered(1))

    def shape(cols, kind=jnp.bfloat16):
        return jax.ShapeDtypeStruct((tok_count, cols), kind)

    return pl.pallas_call(
        body,
        grid=(tok_count // rows,),
        in_specs=[tile(head_cols)] * parts
        + [tile(width), tile(width), whole((1, width))]
        + [fixed(weight_near.shape), fixed(weight_far.shape)],
        out_specs=[tile(width)] * 4
        + [tile(ff)] * 3
        + [whole((1, width))]
        + [tile(head_cols)] * parts,
        out_shape=[
            shape(width),
            shape(width, jnp.float32),
            shape(width),
            shape(width),
            shape(ff),
            shape(ff),
            shape(ff),
            jax.ShapeDtypeStruct((1, width), jnp.float32),
        ]
        + [shape(head_cols)] * parts,
        scratch_shapes=[
            pltpu.VMEM((width, ff), jnp.bfloat16),
            pltpu.VMEM((width, ff), jnp.bfloat16),
            pltpu.VMEM((width, ff), jnp.bfloat16),
            pltpu.VMEM((width, inner), jnp.bfloat16),
        ],
        name="layer",
    )(*att, source, cot, gain[None, :], weight_near, weight_far)


SLOTS = (0, 2, 1, 3)


def weight_grads(side, h_two, d_first, d_second, cot, hidden, d_low, att, gain_grad, wide):
    _, width = h_two.shape
    hid = hidden.shape[1] // len(SLOTS)
    head_cols = att[0].shape[1]
    both = tuple(att[r] for r in SLOTS[2 * side : 2 * side + 2])
    here = slice(2 * side * hid, (2 * side + 2) * hid)

    def body(h_ref, f_ref, s_ref, c_ref, u_ref, l_ref, a_ref, b_ref, g_ref, out_ref):
        sides = jnp.concatenate([f_ref[:, here], s_ref[:, here]], axis=1)
        full = tn_dot(h_ref[...], sides).astype(jnp.bfloat16)
        for s in range(2):
            out_ref[s, :, :hid] = full[:, s * hid : (s + 1) * hid]
            out_ref[s, :, hid : 2 * hid] = full[:, (2 + s) * hid : (3 + s) * hid]
        full = tn_dot(c_ref[...], u_ref[:, here]).astype(jnp.bfloat16)
        heads = tn_dot(l_ref[...], jnp.concatenate([a_ref[...], b_ref[...]], axis=1))
        heads = heads.astype(jnp.bfloat16)
        gain_col = jnp.transpose(jnp.broadcast_to(g_ref[...], (128, width))).astype(jnp.bfloat16)
        at = 3 * hid
        for s in range(2):
            out_ref[s, :, 2 * hid : at] = full[:, s * hid : (s + 1) * hid]
            out_ref[s, :, at : at + head_cols] = heads[:, s * head_cols : (s + 1) * head_cols]
            out_ref[s, :, at + head_cols :] = gain_col[:, : wide - at - head_cols]

    return pl.pallas_call(
        body,
        out_shape=jax.ShapeDtypeStruct((2, width, wide), jnp.bfloat16),
        name="weight_grads",
    )(h_two, d_first, d_second, cot, hidden, d_low, *both, gain_grad)


def back_to_width(d_qkv, weight, place, slots, share):
    width, cols = weight.shape
    first, stride = slots[0], slots[1] - slots[0]

    def body(place_ref, d_ref, w_ref, out_ref):
        out_ref[0] = nt_dot(d_ref[...], w_ref[...]).astype(jnp.bfloat16)

    return pl.pallas_call(
        body,
        grid_spec=pltpu.PrefetchScalarGridSpec(
            num_scalar_prefetch=1,
            grid=(len(slots),),
            in_specs=[
                pl.BlockSpec((share, cols), lambda i, at: (at[0] ^ (first + stride * i), 0)),
                whole(weight.shape),
            ],
            out_specs=pl.BlockSpec((1, share, width), lambda i, at: (i, 0, 0)),
        ),
        out_shape=jax.ShapeDtypeStruct((len(slots), share, width), jnp.bfloat16),
        name="back_to_width",
    )(place, d_qkv, weight)


def share_rows(mine, place, kind=None):
    other = swap(mine, "tensor", 2)
    beside = swap(mine, "tensor", 1)
    across = swap(other, "tensor", 1)
    return assemble([mine, beside, other, across], place, kind)


def layer_shards(
    tokens, lengths, attn_gain, qkv_weight, out_weight, mlp_gain, up_weight, down_weight, cotangent
):
    tok_count, _ = tokens.shape
    parts = lax.axis_size("tensor")
    share = tok_count // parts
    rank = lax.axis_index("tensor").astype(jnp.int32)
    place = rank[None]
    dp_place = lax.axis_index("dp").astype(jnp.int32)[None]
    rows = qkv_weight.shape[0]
    head_cols = qkv_weight.shape[2]
    heads_dev = head_cols // HD
    hid = up_weight.shape[2]
    used = 3 * hid + head_cols
    wide = used // 128 * 128 + 128

    qkv_own = qkv_weight.reshape(rows, 3 * head_cols)
    qkv_own, up_weight, down_weight, out_weight = lax.optimization_barrier(
        (qkv_own, up_weight, down_weight, out_weight)
    )
    qkv_far = gather_far(qkv_own)
    qkv_flat = assemble(gather_near(qkv_far), dp_place)
    packed = jnp.concatenate(
        [
            up_weight.reshape(rows, 2 * hid),
            down_weight.T,
            out_weight.T,
            jnp.zeros((rows, wide - used), jnp.bfloat16),
        ],
        axis=1,
    )
    paired = jnp.stack([packed, swap(packed, "tensor", 2)])
    paired, _ = lax.optimization_barrier((paired, qkv_far))
    paired_far = gather_far(paired)

    segment, position = row_layout(lengths[0], tok_count)
    tables = rotary_tables(position, HD)
    h_one = (normalize(tokens.astype(jnp.float32))[0] * attn_gain).astype(jnp.bfloat16)
    seg_col = jnp.broadcast_to(segment[:, None], (tok_count, TILE // 2))
    seg_row = segment[None, :]
    first, last = tile_ranges(lengths[0], tok_count)
    query, key, value = project_heads(h_one, qkv_flat, tables, heads_dev)
    paired_far, query = lax.optimization_barrier((paired_far, query))
    pieces = gather_near(paired_far)
    *sent, attended_wide, log_total = attend(
        first, last, place, query, key, value, seg_col, seg_row, parts
    )
    weight_near = assemble(pieces, dp_place)
    weight_far = swap(weight_near, "tensor", 1)
    att = [sent[0]] + [swap(sent[r], "tensor", r) for r in range(1, parts)]
    my_tokens = lax.dynamic_slice_in_dim(tokens, rank * share, share, 0)
    my_cot = lax.dynamic_slice_in_dim(cotangent, rank * share, share, 0)
    out, d_mid, d_low, h_two, hidden, d_first, d_second, gain_two, *d_sent = layer(
        att, my_tokens, my_cot, mlp_gain, weight_near, weight_far, hid
    )
    d_att = [d_sent[0]] + [swap(d_sent[r], "tensor", r) for r in range(1, parts)]
    output = share_rows(out, place)

    grads_in = (h_two, d_first, d_second, my_cot, hidden, d_low, att, gain_two, wide)
    grads_far = weight_grads(1, *grads_in)
    grads_near = weight_grads(0, *grads_in)
    grads_come = swap(grads_far, "tensor", 1)
    chip_sent = grads_near[1].astype(jnp.float32) + grads_come[1].astype(jnp.float32)
    chip_sent, d_att = lax.optimization_barrier((chip_sent.astype(jnp.bfloat16), d_att))
    column_come = swap(chip_sent, "tensor", 2)

    shared = (first, last, place, query, key, value, seg_col, seg_row)
    shared = (*shared, d_att, attended_wide, log_total, tables)
    d_qkv = attend_grad(*shared, 0, ())
    d_qkv, column_come = lax.optimization_barrier((d_qkv, column_come))
    column = grads_near[0].astype(jnp.float32) + grads_come[0].astype(jnp.float32)
    column = (column + column_come.astype(jnp.float32)).astype(jnp.bfloat16)
    column_near, column_come = reduce_near(column, dp_place)
    d_qkv = attend_grad(*shared, heads_dev - 1, (d_qkv,))
    d_far = back_to_width(d_qkv, qkv_flat, place, (1, 3), share)
    d_near = back_to_width(d_qkv, qkv_flat, place, (0, 2), share)
    d_side = swap(d_far, "tensor", 1)
    d_sent = d_near[1].astype(jnp.float32) + d_side[1].astype(jnp.float32)
    d_sent, d_qkv = lax.optimization_barrier((d_sent.astype(jnp.bfloat16), d_qkv))
    d_come = swap(d_sent, "tensor", 2)
    qkv_total = jnp.einsum("td,tf->df", h_one, d_qkv, preferred_element_type=jnp.float32)
    qkv_near, qkv_come = reduce_near(qkv_total.astype(jnp.bfloat16), dp_place)
    normed_one, factor_one = normalize(my_tokens.astype(jnp.float32))
    d_h_one = d_near[0].astype(jnp.float32) + d_side[0].astype(jnp.float32)
    d_h_one = d_h_one + d_come.astype(jnp.float32)
    tokens_grad = d_mid + norm_back(d_h_one, normed_one, factor_one, attn_gain)
    tokens_grad = share_rows(tokens_grad.astype(jnp.bfloat16), place, jnp.float32)
    reduced = reduce_far(column_near, column_come)
    up_grad = reduced[:, : 2 * hid].reshape(rows, 2, hid)
    down_grad = reduced[:, 2 * hid : 3 * hid].T
    out_grad = reduced[:, 3 * hid : used].T
    mlp_gain_grad = reduced[:, used]
    qkv_grad = reduce_far(qkv_near, qkv_come)
    gain_one = jnp.sum(qkv_grad * qkv_own.astype(jnp.float32), axis=1)
    gain_one = gain_one + sum(swap(gain_one, "tensor", r) for r in range(1, parts))
    attn_gain_grad = gain_one / lax.dynamic_slice_in_dim(attn_gain, dp_place[0] * rows, rows, 0)
    qkv_grad = qkv_grad.reshape(rows, 3, head_cols)
    return (
        output,
        tokens_grad,
        attn_gain_grad,
        qkv_grad,
        out_grad,
        mlp_gain_grad,
        up_grad,
        down_grad,
    )


def solution(mesh):
    in_specs = (
        P("dp", None),
        P("dp", None),
        P(),
        P("dp", None, "tensor"),
        P("tensor", "dp"),
        P(),
        P("dp", None, "tensor"),
        P("tensor", "dp"),
        P("dp", None),
    )
    out_specs = (
        P("dp", None),
        P("dp", None),
        P("dp"),
        P("dp", None, "tensor"),
        P("tensor", "dp"),
        P("dp"),
        P("dp", None, "tensor"),
        P("tensor", "dp"),
    )
    return jax.shard_map(layer_shards, mesh=mesh, in_specs=in_specs, out_specs=out_specs, check_vma=False)
```
